128 devices in a mesh: blk: 32 (over x, y, core), grp: 4 (over z).
Axes of the slice: x: 4, y: 4, z: 4, core: 2. Of those that a mesh axis runs over, the one named last changes fastest.
Arguments:
- tensor_blocks: bfloat16 [4608, 64, 4096], P(('blk', 'grp')), may hold values from 0 to 1
- block_coords: int32 [3, 4608], P(None, ('blk', 'grp')), may hold values from 0 to 255, as said below
- block_count: int32 [128], P(('blk', 'grp')), may hold values from 1 to 36, as said below
- row_owner: int32 [3, 256], replicated, may hold values from 0 to 255, as said below
- factors: float32 [3, 16384, 256], P(None, ('blk', 'grp')), may hold values from -2.4 to 2.4
- moment1: float32 [16384, 256], P(('blk', 'grp')), may hold values from -1.8 to 1.8
- moment2: float32 [16384, 256], P(('blk', 'grp')), may hold values from 0.01 to 1
Outputs:
- new_factor: float32 [16384, 256], P(('blk', 'grp'))
- new_moment1: float32 [16384, 256], P(('blk', 'grp'))
- new_moment2: float32 [16384, 256], P(('blk', 'grp'))
The draws below stay inside these ranges and needn't reach their ends.
Inputs may be any that keep to these rules, and one draw needn't show every extreme that they name: `row_owner`: for each mode a permutation; storage position p lies on device p // 2 of blk+grp. `block_coords`: of the 108 row blocks named by one device's slots, at most 2 have positions on any one device, and exactly 2 on some device; of the 36 first-mode row blocks named by one device's slots, at most 1 have positions on any one device, and exactly 1 on some device. `block_count`: some device has all slots live.
All inputs are finite; a program needn't handle non-finite values.
Results may differ from the reference program's by a relative error of at most 0.0012.
Values may be sent and summed in bfloat16 or wider, within the bound.
A program may use at most 128 MiB of HBM per device.

```python
import math
import jax
import jax.numpy as jnp
from jax import lax

E = 64
R = 256
BLK_DEV = 36
ROWB = 2
NBLK = 4608
NROWB = 256
ROWS = 16384
CAP = 2
CAP0 = 1
DEVICES = 128


def common_tables(key):
    perms = jnp.stack([jax.random.permutation(jax.random.fold_in(key, 11 + m), NROWB) for m in range(3)]).astype(jnp.int32)
    inverse = jnp.argsort(perms, axis=1).astype(jnp.int32)
    spread = DEVICES * CAP

    def one_device(device):
        base = jax.random.fold_in(jax.random.fold_in(key, 29), device)
        key_first, key_pool, key_order, key_slot, key_score, key_rest = jax.random.split(base, 6)
        first = jax.random.randint(key_first, (), 0, DEVICES)
        pool = (first + 1 + jnp.repeat(jnp.arange(DEVICES - 1), CAP0)) % DEVICES
        pool = jax.random.permutation(key_pool, pool)[:BLK_DEV - CAP0]
        dests_first = jnp.concatenate([jnp.full((CAP0,), first, jnp.int32), pool.astype(jnp.int32)])
        dests_first = jax.random.permutation(key_order, dests_first).astype(jnp.int32)
        counts_first = jnp.sum((dests_first[:, None] == jnp.arange(DEVICES)[None, :]).astype(jnp.int32), axis=0)
        cand_dev = jnp.repeat(jnp.arange(DEVICES, dtype=jnp.int32), CAP)
        cand_rank = jnp.tile(jnp.arange(CAP, dtype=jnp.int32), DEVICES)
        valid = cand_rank >= jnp.take(counts_first, cand_dev)
        scores = jax.random.permutation(key_score, spread).astype(jnp.int32)
        scores = jnp.where(valid, scores, scores + 2 * spread)
        scores = jnp.where(valid & (cand_dev == first), scores - 2 * spread, scores)
        chosen = jnp.take(cand_dev, jnp.argsort(scores)[:2 * BLK_DEV])
        chosen = jax.random.permutation(key_rest, chosen).astype(jnp.int32)
        dests = jnp.concatenate([dests_first, chosen])
        slot = jax.random.randint(key_slot, (3 * BLK_DEV,), 0, ROWB)
        return (dests * ROWB + slot).astype(jnp.int32)
    spots = jax.vmap(one_device)(jnp.arange(DEVICES))
    spots = spots.reshape(DEVICES, 3, BLK_DEV).transpose(1, 0, 2).reshape(3, NBLK)
    coords = jnp.take_along_axis(inverse, spots, axis=1)
    return (perms, coords)


def draw_row_owner(key, part):
    return common_tables(key)[0]


def draw_block_coords(key, part):
    return common_tables(key)[1]


def draw_block_count(key, part):
    key_counts, key_full = jax.random.split(jax.random.fold_in(key, 53))
    counts = jax.random.randint(key_counts, (DEVICES,), max(1, BLK_DEV // 4), BLK_DEV + 1)
    fullest = jax.random.randint(key_full, (), 0, DEVICES)
    return counts.at[fullest].set(BLK_DEV).astype(jnp.int32)


def level_of(rng, extent, pieces, smallest, high):
    def one(axis_at, parts):
        draws = jax.random.uniform(jax.random.fold_in(jax.random.fold_in(rng, 6), axis_at), (parts,), jnp.float32, smallest / len(pieces), high / len(pieces))
        return jnp.repeat(jnp.exp(draws), extent[axis_at] // parts).reshape((-1,) + (1,) * (len(extent) - axis_at - 1))

    factor_of = one(*pieces[0])
    for cut in pieces[1:]:
        factor_of = factor_of * one(*cut)
    return factor_of


def normal_values(stream_key, shape, width, bound, pieces=(), held_as=jnp.bfloat16):
    entries = width * jax.random.normal(stream_key, shape, jnp.float32)
    if pieces:
        entries = entries * level_of(stream_key, shape, pieces, -0.22, 0.18)
    return jnp.clip(entries, -bound, bound).astype(held_as)


def setup_inputs(seed: int = 0) -> dict:
    streams_of = jax.random.split(jax.random.key(seed), 8)
    return {
        "tensor_blocks": jnp.clip(1.0 * jax.random.uniform(streams_of[0], (NBLK, E, E * E), jnp.float32) ** level_of(streams_of[0], (NBLK, E, E * E), ((0, 128),), -0.2, 0.2), 0.0, 1.0).astype(jnp.bfloat16),
        "block_coords": draw_block_coords(jax.random.fold_in(streams_of[7], 71), 0),
        "block_count": draw_block_count(jax.random.fold_in(streams_of[7], 71), 0),
        "row_owner": draw_row_owner(jax.random.fold_in(streams_of[7], 71), 0),
        "factors": normal_values(streams_of[4], (3, ROWS, R), 0.4, 2.4, ((1, 128),), jnp.float32),
        "moment1": normal_values(streams_of[5], (ROWS, R), 0.3, 1.8, ((0, 128),), jnp.float32),
        "moment2": jnp.clip(jnp.exp(math.log(1.0) - 4.6051702 * jax.random.uniform(streams_of[6], (ROWS, R), jnp.float32) ** level_of(streams_of[6], (ROWS, R), ((0, 128),), -0.2, 0.2)), 0.01, 1.0),
    }


def reference(tensor_blocks, block_coords, block_count, row_owner, factors, moment1, moment2):
    nblk = tensor_blocks.shape[0]
    slots = jnp.arange(nblk, dtype=jnp.int32)
    counts = jnp.take(block_count, slots // BLK_DEV)
    live = (slots % BLK_DEV < counts).astype(jnp.float32)
    positions = jnp.stack([jnp.take(row_owner[m], block_coords[m]) for m in range(3)], axis=1).astype(jnp.int32)

    def step(grad, item):
        block, pos, alive = item
        rows = [lax.dynamic_slice_in_dim(factors[m], (pos[m] * E).astype(jnp.int32), E, 0).astype(jnp.bfloat16) for m in range(3)]
        pair = (rows[1].astype(jnp.float32)[:, None, :] * rows[2].astype(jnp.float32)[None, :, :]).reshape(E * E, R).astype(jnp.bfloat16)
        model = lax.dot_general(rows[0], pair, (((1,), (1,)), ((), ())), preferred_element_type=jnp.float32)
        resid = ((jax.nn.sigmoid(model) - block.astype(jnp.float32)) * alive).astype(jnp.bfloat16)
        part = jnp.dot(resid, pair, preferred_element_type=jnp.float32)
        start = (pos[0] * E).astype(jnp.int32)
        old = lax.dynamic_slice_in_dim(grad, start, E, 0)
        return (lax.dynamic_update_slice_in_dim(grad, old + part, start, 0), None)
    grad, _ = lax.scan(step, jnp.zeros((ROWS, R), jnp.float32), (tensor_blocks, positions, live))
    new_moment1 = 0.9 * moment1 + 0.1 * grad
    new_moment2 = 0.999 * moment2 + 0.001 * grad * grad
    new_factor = factors[0] - 0.02 * (new_moment1 / (1.0 - 0.9 ** 8)) / (jnp.sqrt(new_moment2 / (1.0 - 0.999 ** 8)) + 1e-08)
    return (new_factor, new_moment1, new_moment2)
```

```python
import functools

import jax
import jax.numpy as jnp
from jax import lax
from jax.experimental import pallas as pl
from jax.experimental.pallas import tpu as pltpu
from jax.sharding import PartitionSpec as P

AXES = ("blk", "grp")


def block_kernel(edge, chunk, where_ref, count_ref, block_ref, a_ref, b_ref, c_ref, zero_ref, out_ref):
    slot = pl.program_id(0)

    @pl.when(slot < count_ref[0])
    def _():
        half_a = a_ref[0] * jnp.bfloat16(0.5)
        rows_c = c_ref[0]
        rank = rows_c.shape[1]
        total = jnp.zeros((edge, rank), jnp.float32)
        for step in range(edge // chunk):
            pair = jnp.concatenate(
                [b_ref[0, pl.ds(step * chunk + j, 1), :] * rows_c for j in range(chunk)], axis=0
            )
            model = lax.dot_general(
                half_a, pair, (((1,), (1,)), ((), ())), preferred_element_type=jnp.float32
            )
            width = chunk * edge
            observed = block_ref[0, :, step * width : (step + 1) * width].astype(jnp.float32)
            resid = (0.5 * jnp.tanh(model) + (0.5 - observed)).astype(jnp.bfloat16)
            total = total + jnp.dot(resid, pair, preferred_element_type=jnp.float32)
        out_ref[0] = total

    @pl.when(slot >= count_ref[0])
    def _():
        out_ref[...] = jnp.zeros_like(out_ref)


def block_gradients(tensor_blocks, table, where, count, zeros):
    slots, edge, merged = tensor_blocks.shape
    rank = table.shape[2]
    spec = lambda m: pl.BlockSpec((1, edge, rank), lambda s, w, n: (w[m, s], 0, 0))
    return pl.pallas_call(
        functools.partial(block_kernel, edge, 8),
        out_shape=jax.ShapeDtypeStruct(zeros.shape, jnp.float32),
        grid_spec=pltpu.PrefetchScalarGridSpec(
            num_scalar_prefetch=2,
            grid=(slots,),
            in_specs=[
                pl.BlockSpec((1, edge, merged), lambda s, w, n: (s, 0, 0)),
                spec(0),
                spec(1),
                spec(2),
                pl.BlockSpec(memory_space=pl.ANY),
            ],
            out_specs=pl.BlockSpec((1, edge, rank), lambda s, w, n: (w[3, s], 0, 0)),
        ),
        input_output_aliases={6: 0},
        compiler_params=pltpu.CompilerParams(
            dimension_semantics=("arbitrary",), vmem_limit_bytes=48 << 20
        ),
        cost_estimate=pl.CostEstimate(
            flops=4 * slots * edge * merged * rank,
            bytes_accessed=2 * slots * edge * (merged + 5 * rank),
            transcendentals=slots * edge * merged,
        ),
    )(where, count, tensor_blocks, table, table, table, zeros)


def per_device(tensor_blocks, block_coords, block_count, row_owner, factors, moment1, moment2):
    slot_count, edge, _ = tensor_blocks.shape
    modes, _, rank = factors.shape
    devices = lax.axis_size(AXES)
    local_blocks = moment1.shape[0] // edge
    blocks = devices * local_blocks
    pos = jnp.take_along_axis(row_owner, block_coords, axis=1)
    mode = jnp.arange(modes, dtype=jnp.int32)[:, None]
    where = (pos // local_blocks) * (modes * local_blocks) + mode * local_blocks + pos % local_blocks
    where = jnp.concatenate([where, pos[:1]], axis=0)
    table = lax.all_gather(factors.astype(jnp.bfloat16), AXES, axis=0, tiled=False)
    table = table.reshape(modes * blocks, edge, rank)
    zeros = jnp.zeros((blocks, edge, rank), jnp.float32)
    parts = block_gradients(tensor_blocks, table, where, block_count, zeros)
    grad = lax.psum_scatter(
        parts.reshape(blocks * edge, rank), AXES, scatter_dimension=0, tiled=True
    )
    new_moment1 = 0.9 * moment1 + 0.1 * grad
    new_moment2 = 0.999 * moment2 + 0.001 * grad * grad
    new_factor = factors[0] - 0.02 * (new_moment1 / (1.0 - 0.9**8)) / (
        jnp.sqrt(new_moment2 / (1.0 - 0.999**8)) + 1e-08
    )
    return (new_factor, new_moment1, new_moment2)


def solution(mesh):
    return jax.shard_map(
        per_device,
        mesh=mesh,
        in_specs=(
            P(AXES, None, None),
            P(None, AXES),
            P(AXES),
            P(),
            P(None, AXES, None),
            P(AXES, None),
            P(AXES, None),
        ),
        out_specs=(P(AXES, None), P(AXES, None), P(AXES, None)),
        check_vma=False,
    )
```

```python
import functools

import jax
import jax.numpy as jnp
from jax import lax
from jax.experimental import pallas as pl
from jax.experimental.pallas import tpu as pltpu
from jax.sharding import PartitionSpec as P

AXES = ("blk", "grp")
MESH = pl.DeviceIdType.MESH
RING = 4
ORDERS = ((0, 1, 2), (1, 2, 0), (2, 0, 1))


class Place:
    def __init__(self):
        blk = lax.axis_index("blk")
        self.coord = [lax.div(blk, 8), lax.rem(lax.div(blk, 2), 4), lax.axis_index("grp")]
        self.core = lax.rem(blk, 2)

    @staticmethod
    def device(coord, core):
        return (coord[0] * 8 + coord[1] * 2 + core, coord[2])

    def partner(self):
        return self.device(self.coord, 1 - self.core)

    def along(self, axis, step):
        return lax.rem(self.coord[axis] + (RING + step), RING)

    def neighbour(self, axis, step):
        coord = list(self.coord)
        coord[axis] = self.along(axis, step)
        return self.device(coord, self.core)

    def greet(self):
        barrier = pltpu.get_barrier_semaphore()
        peers = [self.neighbour(axis, step) for axis in range(3) for step in (1, -1)]
        for peer in peers + [self.partner()]:
            pl.semaphore_signal(barrier, inc=1, device_id=peer, device_id_type=MESH)
        pl.semaphore_wait(barrier, 7)


def remote(src, dst, send, recv, device):
    return pltpu.make_async_remote_copy(
        src_ref=src, dst_ref=dst, send_sem=send, recv_sem=recv, device_id=device, device_id_type=MESH
    )


def gather_kernel(own_ref, table_ref, cast_ref, local_sem, own_sem, send, recv, pair_send, pair_recv):
    place = Place()
    x, y, z = place.coord
    core = place.core
    other = 1 - core
    half_rows = cast_ref.shape[1] // 2

    def region(part, stage, value, half, side):
        index = list(place.coord)
        for axis in ORDERS[part][:stage]:
            index[axis] = slice(None)
        index[ORDERS[part][stage]] = value
        return table_ref.at[
            index[0], index[1], side, index[2], part, half * half_rows : (half + 1) * half_rows
        ]

    def arrived(part, stage, way, k, side):
        axis = ORDERS[part][stage]
        step = -1 if way == 0 else 1
        value = place.along(axis, step if k < 2 else 2)
        return region(part, stage, value, way if k != 1 else 1 - way, side)

    def outgoing(part, stage, way, k):
        axis = ORDERS[part][stage]
        half = way if k != 1 else 1 - way
        if k < 2:
            dst = region(part, stage, place.coord[axis], half, core)
            src = dst
            if stage == 0:
                src = cast_ref.at[part, half * half_rows : (half + 1) * half_rows]
        else:
            dst = src = arrived(part, stage, way, 0, core)
        device = place.neighbour(axis, 1 if way == 0 else -1)
        return remote(src, dst, send.at[part, stage, way, k], recv.at[part, stage, way, k], device)

    def incoming(part, stage, way, k):
        ref = arrived(part, stage, way, k, core)
        axis = ORDERS[part][stage]
        device = place.neighbour(axis, 1 if way == 0 else -1)
        return remote(ref, ref, send.at[part, stage, way, k], recv.at[part, stage, way, k], device)

    def across(part, stage, way, k, side):
        ref = arrived(part, stage, way, k, side)
        at = (part, stage, way, k)
        return remote(ref, ref, pair_send.at[at], pair_recv.at[at], place.partner())

    cast_ref[...] = own_ref[...].astype(cast_ref.dtype)
    place.greet()
    steps = [(part, way) for part in range(3) for way in range(2)]
    for k in range(2):
        for part, way in steps:
            outgoing(part, 0, way, k).start()
    mine = pltpu.make_async_copy(cast_ref, table_ref.at[x, y, core, z], local_sem)
    mine.start()
    own = remote(cast_ref, table_ref.at[x, y, core, z], own_sem.at[0], own_sem.at[1], place.partner())
    own.start()
    mine.wait()
    for stage in range(3):
        for k in range(3):
            for part in range(3):
                for way in range(2):
                    incoming(part, stage, way, k).wait_recv()
                    if k == 0:
                        outgoing(part, stage, way, 2).start()
                    across(part, stage, way, k, core).start()
                if k == 2 and stage < 2:
                    for way in range(2):
                        outgoing(part, stage + 1, way, 0).start()
                        outgoing(part, stage + 1, way, 1).start()
    own.wait_send()
    theirs = table_ref.at[x, y, other, z]
    remote(theirs, theirs, own_sem.at[0], own_sem.at[1], place.partner()).wait_recv()
    for stage in range(3):
        for k in range(3):
            for part, way in steps:
                outgoing(part, stage, way, k).wait_send()
                across(part, stage, way, k, core).wait_send()
                across(part, stage, way, k, other).wait_recv()


def gather_rows(factors):
    modes, rows, rank = factors.shape
    return pl.pallas_call(
        gather_kernel,
        out_shape=jax.ShapeDtypeStruct((4, 4, 2, 4, modes, rows, rank), jnp.bfloat16),
        in_specs=[pl.BlockSpec(memory_space=pltpu.VMEM)],
        out_specs=pl.BlockSpec(memory_space=pl.ANY),
        scratch_shapes=[
            pltpu.VMEM((modes, rows, rank), jnp.bfloat16),
            pltpu.SemaphoreType.DMA,
            pltpu.SemaphoreType.DMA((2,)),
            pltpu.SemaphoreType.DMA((3, 3, 2, 3)),
            pltpu.SemaphoreType.DMA((3, 3, 2, 3)),
            pltpu.SemaphoreType.DMA((3, 3, 2, 3)),
            pltpu.SemaphoreType.DMA((3, 3, 2, 3)),
        ],
        compiler_params=pltpu.CompilerParams(collective_id=0, has_side_effects=True),
    )(factors)


def block_kernel(slots, edge, chunk, coords_ref, owner_ref, count_ref, block_ref, a_ref, b_ref, c_ref, out_ref, slot_ref):
    slot = pl.program_id(0)

    @pl.when(slot == 0)
    def _():
        @pl.loop(0, slot_ref.shape[0])
        def _(p):
            slot_ref[p] = slots

        @pl.loop(0, slots)
        def _(s):
            slot_ref[owner_ref[0, coords_ref[0, s]]] = s

    @pl.when(slot < count_ref[0])
    def _():
        half_a = a_ref[0] * jnp.bfloat16(0.5)
        rows_c = c_ref[0]
        rank = rows_c.shape[1]
        total = jnp.zeros((edge, rank), jnp.float32)
        for step in range(edge // chunk):
            pair = jnp.concatenate(
                [b_ref[0, pl.ds(step * chunk + j, 1), :] * rows_c for j in range(chunk)], axis=0
            )
            model = lax.dot_general(
                half_a, pair, (((1,), (1,)), ((), ())), preferred_element_type=jnp.float32
            )
            width = chunk * edge
            observed = block_ref[0, :, step * width : (step + 1) * width].astype(jnp.float32)
            resid = (0.5 * jnp.tanh(model) + (0.5 - observed)).astype(jnp.bfloat16)
            total = total + jnp.dot(resid, pair, preferred_element_type=jnp.float32)
        out_ref[0] = total

    @pl.when(slot >= count_ref[0])
    def _():
        out_ref[...] = jnp.zeros_like(out_ref)


def block_gradients(tensor_blocks, table, coords, owner, count, positions, local_blocks):
    slots, edge, merged = tensor_blocks.shape
    modes, _ = coords.shape
    rank = table.shape[2]

    def rows_of(m):
        def index(s, coords_ref, owner_ref, count_ref):
            pos = owner_ref[m, coords_ref[m, jnp.minimum(s, slots - 1)]]
            device = lax.div(pos, local_blocks)
            return ((device * modes + m) * local_blocks + lax.rem(pos, local_blocks), 0, 0)

        return pl.BlockSpec((1, edge, rank), index)

    return pl.pallas_call(
        functools.partial(block_kernel, slots, edge, 8),
        out_shape=(
            jax.ShapeDtypeStruct((slots + 1, edge, rank), jnp.float32),
            jax.ShapeDtypeStruct((positions,), jnp.int32),
        ),
        grid_spec=pltpu.PrefetchScalarGridSpec(
            num_scalar_prefetch=3,
            grid=(slots + 1,),
            in_specs=[
                pl.BlockSpec((1, edge, merged), lambda s, *_: (jnp.minimum(s, slots - 1), 0, 0)),
                rows_of(0),
                rows_of(1),
                rows_of(2),
            ],
            out_specs=(
                pl.BlockSpec((1, edge, rank), lambda s, *_: (s, 0, 0)),
                pl.BlockSpec(memory_space=pltpu.SMEM),
            ),
        ),
        compiler_params=pltpu.CompilerParams(
            dimension_semantics=("arbitrary",), vmem_limit_bytes=48 << 20
        ),
        cost_estimate=pl.CostEstimate(
            flops=4 * slots * edge * merged * rank,
            bytes_accessed=2 * slots * edge * (merged + 5 * rank),
            transcendentals=slots * edge * merged,
        ),
    )(coords, owner, count, tensor_blocks, table, table, table)


CUTS = (((0, 88), (0, 128)), ((0, 88), (128, 256)), ((88, 128), (0, 256)))
SPLITS = ((48, 40), (48, 40), (24, 16))


def half_shape(part, stage):
    (r0, r1), (c0, c1) = CUTS[part]
    sizes = [RING, RING, RING]
    for axis in ORDERS[part][: stage + 1]:
        sizes[axis] = None
    if stage < 2:
        sizes[ORDERS[part][stage + 1]] = 2
        rows = r1 - r0
    else:
        rows = SPLITS[part][0]
    return tuple(n for n in sizes if n is not None) + (rows, c1 - c0)


def scatter_kernel(slot_ref, parts_ref, grad_ref, acc, outbox, inbox, *rest):
    buffers = rest[:9]
    send, recv, pair_send, pair_recv = rest[9:]
    place = Place()
    edge = parts_ref.shape[1]

    def region(ref, part, stage, k, half):
        order = ORDERS[part]
        (r0, r1), (c0, c1) = CUTS[part]
        index = [slice(None)] * 3
        for axis in order[:stage]:
            index[axis] = 0
        index[order[stage]] = k
        if half is not None:
            if stage < 2:
                index[order[stage + 1]] = slice(2 * half, 2 * half + 2)
            else:
                cut = r0 + SPLITS[part][0]
                r0, r1 = (r0, cut) if half == 0 else (cut, r1)
        return ref.at[index[0], index[1], index[2], r0:r1, c0:c1]

    def half_of(way, k):
        return way if k != 1 else 1 - way

    def landing(part, stage, way, k):
        ref = buffers[part * 3 + stage].at[way, k]
        if stage == 2:
            ref = ref.at[0 : SPLITS[part][half_of(way, k)]]
        return ref

    def outgoing(part, stage, way, k):
        offset = 2 if k == 0 else (3 if way == 0 else 1)
        src = region(acc, part, stage, offset, half_of(way, k))
        device = place.neighbour(ORDERS[part][stage], -1 if way == 0 else 1)
        at = (part, stage, way, k)
        return remote(src, landing(part, stage, way, k), send.at[at], recv.at[at], device)

    def take(part, stage, way, k):
        outgoing(part, stage, way, k).wait_recv()
        offset = (3 if way == 0 else 1) if k == 0 else 0
        target = region(acc, part, stage, offset, half_of(way, k))
        target[...] = target[...] + landing(part, stage, way, k)[...]

    def across(part, k):
        at = (part, k)
        return remote(
            region(outbox, part, 0, k, None),
            region(inbox, part, 0, k, None),
            pair_send.at[at],
            pair_recv.at[at],
            place.partner(),
        )

    def take_across(part, k):
        across(part, k).wait_recv()
        target = region(acc, part, 0, k, None)
        target[...] = target[...] + region(inbox, part, 0, k, None)[...]

    def spread(ref, core):
        @pl.loop(0, RING**3)
        def _(r):
            step = (lax.div(r, 16), lax.rem(lax.div(r, 4), 4), lax.rem(r, 4))
            blk, grp = place.device(
                [lax.rem(v + s, RING) for v, s in zip(place.coord, step)], core
            )
            first = (blk * 4 + grp) * 2
            for j in range(2):
                ref[step[0], step[1], step[2], j * edge : (j + 1) * edge, :] = parts_ref[
                    slot_ref[first + j]
                ]

    spread(outbox, 1 - place.core)
    place.greet()
    for k in (2, 3, 1, 0):
        for part in range(3):
            across(part, k).start()
    spread(acc, place.core)
    for part in range(3):
        take_across(part, 2)
        for way in range(2):
            outgoing(part, 0, way, 0).start()
    for part in range(3):
        for way, k in ((0, 3), (1, 1)):
            take_across(part, k)
            outgoing(part, 0, way, 1).start()
    for stage in range(3):
        for part in range(3):
            for way in range(2):
                take(part, stage, way, 0)
                outgoing(part, stage, way, 2).start()
        if stage == 0:
            for part in range(3):
                take_across(part, 0)
        for part in range(3):
            for k in (1, 2):
                for way in range(2):
                    take(part, stage, way, k)
            if stage < 2:
                for k in range(2):
                    for way in range(2):
                        outgoing(part, stage + 1, way, k).start()
    grad_ref[...] = acc[0, 0, 0]
    for part in range(3):
        for k in range(4):
            across(part, k).wait_send()
        for stage in range(3):
            for way in range(2):
                for k in range(3):
                    outgoing(part, stage, way, k).wait_send()


def scatter_gradients(parts, slot_of):
    edge, rank = parts.shape[1:]
    dense = (RING, RING, RING, 2 * edge, rank)
    buffers = [
        pltpu.VMEM((2, 3) + half_shape(part, stage), jnp.float32)
        for part in range(3)
        for stage in range(3)
    ]
    return pl.pallas_call(
        scatter_kernel,
        out_shape=jax.ShapeDtypeStruct((2 * edge, rank), jnp.float32),
        in_specs=[
            pl.BlockSpec(memory_space=pltpu.SMEM),
            pl.BlockSpec(memory_space=pltpu.VMEM),
        ],
        out_specs=pl.BlockSpec(memory_space=pltpu.VMEM),
        scratch_shapes=[pltpu.VMEM(dense, jnp.float32)] * 3
        + buffers
        + [
            pltpu.SemaphoreType.DMA((3, 3, 2, 3)),
            pltpu.SemaphoreType.DMA((3, 3, 2, 3)),
            pltpu.SemaphoreType.DMA((3, 4)),
            pltpu.SemaphoreType.DMA((3, 4)),
        ],
        compiler_params=pltpu.CompilerParams(
            collective_id=1, has_side_effects=True, vmem_limit_bytes=56 << 20
        ),
    )(slot_of, parts)


def per_device(tensor_blocks, block_coords, block_count, row_owner, factors, moment1, moment2):
    edge = tensor_blocks.shape[1]
    modes, local_rows, rank = factors.shape
    local_blocks = local_rows // edge
    positions = lax.axis_size(AXES) * local_blocks
    table = gather_rows(factors).reshape(modes * positions, edge, rank)
    parts, slot_of = block_gradients(
        tensor_blocks, table, block_coords, row_owner, block_count, positions, local_blocks
    )
    grad = scatter_gradients(parts, slot_of)
    new_moment1 = 0.9 * moment1 + 0.1 * grad
    new_moment2 = 0.999 * moment2 + 0.001 * grad * grad
    new_factor = factors[0] - 0.02 * (new_moment1 / (1.0 - 0.9**8)) / (
        jnp.sqrt(new_moment2 / (1.0 - 0.999**8)) + 1e-08
    )
    return (new_factor, new_moment1, new_moment2)


def solution(mesh):
    return jax.shard_map(
        per_device,
        mesh=mesh,
        in_specs=(
            P(AXES, None, None),
            P(None, AXES),
            P(AXES),
            P(),
            P(None, AXES, None),
            P(AXES, None),
            P(AXES, None),
        ),
        out_specs=(P(AXES, None), P(AXES, None), P(AXES, None)),
        check_vma=False,
    )
```

```python
import functools

import jax
import jax.numpy as jnp
from jax import lax
from jax.experimental import pallas as pl
from jax.experimental.pallas import tpu as pltpu
from jax.sharding import PartitionSpec as P

AXES = ("blk", "grp")
MESH = pl.DeviceIdType.MESH
RING = 4
ORDERS = ((0, 1, 2), (1, 2, 0), (2, 0, 1))


class Place:
    def __init__(self):
        blk = lax.axis_index("blk")
        self.coord = [lax.div(blk, 8), lax.rem(lax.div(blk, 2), 4), lax.axis_index("grp")]
        self.core = lax.rem(blk, 2)

    @staticmethod
    def device(coord, core):
        return (coord[0] * 8 + coord[1] * 2 + core, coord[2])

    def partner(self):
        return self.device(self.coord, 1 - self.core)

    def along(self, axis, step):
        return lax.rem(self.coord[axis] + (RING + step), RING)

    def neighbour(self, axis, step):
        coord = list(self.coord)
        coord[axis] = self.along(axis, step)
        return self.device(coord, self.core)

    def greet(self):
        barrier = pltpu.get_barrier_semaphore()
        peers = [self.neighbour(axis, step) for axis in range(3) for step in (1, -1)]
        for peer in peers + [self.partner()]:
            pl.semaphore_signal(barrier, inc=1, device_id=peer, device_id_type=MESH)
        pl.semaphore_wait(barrier, 7)


def remote(src, dst, send, recv, device):
    return pltpu.make_async_remote_copy(
        src_ref=src, dst_ref=dst, send_sem=send, recv_sem=recv, device_id=device, device_id_type=MESH
    )


def gather_kernel(own_ref, table_ref, cast_ref, local_sem, own_sem, send, recv, pair_send, pair_recv):
    place = Place()
    x, y, z = place.coord
    core = place.core
    other = 1 - core
    half_rows = cast_ref.shape[1] // 2

    def region(part, stage, value, half, side):
        index = list(place.coord)
        for axis in ORDERS[part][:stage]:
            index[axis] = slice(None)
        index[ORDERS[part][stage]] = value
        return table_ref.at[
            index[0], index[1], side, index[2], part, half * half_rows : (half + 1) * half_rows
        ]

    def arrived(part, stage, way, k, side):
        axis = ORDERS[part][stage]
        step = -1 if way == 0 else 1
        value = place.along(axis, step if k < 2 else 2)
        return region(part, stage, value, way if k != 1 else 1 - way, side)

    def outgoing(part, stage, way, k):
        axis = ORDERS[part][stage]
        half = way if k != 1 else 1 - way
        if k < 2:
            dst = region(part, stage, place.coord[axis], half, core)
            src = dst
            if stage == 0:
                src = cast_ref.at[part, half * half_rows : (half + 1) * half_rows]
        else:
            dst = src = arrived(part, stage, way, 0, core)
        device = place.neighbour(axis, 1 if way == 0 else -1)
        return remote(src, dst, send.at[part, stage, way, k], recv.at[part, stage, way, k], device)

    def incoming(part, stage, way, k):
        ref = arrived(part, stage, way, k, core)
        axis = ORDERS[part][stage]
        device = place.neighbour(axis, 1 if way == 0 else -1)
        return remote(ref, ref, send.at[part, stage, way, k], recv.at[part, stage, way, k], device)

    def across(part, stage, way, k, side):
        ref = arrived(part, stage, way, k, side)
        at = (part, stage, way, k)
        return remote(ref, ref, pair_send.at[at], pair_recv.at[at], place.partner())

    cast_ref[...] = own_ref[...].astype(cast_ref.dtype)
    place.greet()
    steps = [(part, way) for part in range(3) for way in range(2)]
    for k in range(2):
        for part, way in steps:
            outgoing(part, 0, way, k).start()
    mine = pltpu.make_async_copy(cast_ref, table_ref.at[x, y, core, z], local_sem)
    mine.start()
    own = remote(cast_ref, table_ref.at[x, y, core, z], own_sem.at[0], own_sem.at[1], place.partner())
    own.start()
    mine.wait()
    for stage in range(3):
        for k in range(3):
            for part in range(3):
                for way in range(2):
                    incoming(part, stage, way, k).wait_recv()
                    if k == 0:
                        outgoing(part, stage, way, 2).start()
                    across(part, stage, way, k, core).start()
                if k == 2 and stage < 2:
                    for way in range(2):
                        outgoing(part, stage + 1, way, 0).start()
                        outgoing(part, stage + 1, way, 1).start()
    own.wait_send()
    theirs = table_ref.at[x, y, other, z]
    remote(theirs, theirs, own_sem.at[0], own_sem.at[1], place.partner()).wait_recv()
    for stage in range(3):
        for k in range(3):
            for part, way in steps:
                outgoing(part, stage, way, k).wait_send()
                across(part, stage, way, k, core).wait_send()
                across(part, stage, way, k, other).wait_recv()


def gather_rows(factors):
    modes, rows, rank = factors.shape
    return pl.pallas_call(
        gather_kernel,
        out_shape=jax.ShapeDtypeStruct((4, 4, 2, 4, modes, rows, rank), jnp.bfloat16),
        in_specs=[pl.BlockSpec(memory_space=pltpu.VMEM)],
        out_specs=pl.BlockSpec(memory_space=pl.ANY),
        scratch_shapes=[
            pltpu.VMEM((modes, rows, rank), jnp.bfloat16),
            pltpu.SemaphoreType.DMA,
            pltpu.SemaphoreType.DMA((2,)),
            pltpu.SemaphoreType.DMA((3, 3, 2, 3)),
            pltpu.SemaphoreType.DMA((3, 3, 2, 3)),
            pltpu.SemaphoreType.DMA((3, 3, 2, 3)),
            pltpu.SemaphoreType.DMA((3, 3, 2, 3)),
        ],
        compiler_params=pltpu.CompilerParams(collective_id=0, has_side_effects=True),
    )(factors)


def block_part(edge, chunk, half_a, b_ref, rows_c, block_ref):
    total = jnp.zeros((edge, rows_c.shape[1]), jnp.float32)
    width = chunk * edge
    for step in range(edge // chunk):
        pair = jnp.concatenate(
            [b_ref[pl.ds(step * chunk + j, 1), :] * rows_c for j in range(chunk)], axis=0
        )
        model = lax.dot_general(
            half_a, pair, (((1,), (1,)), ((), ())), preferred_element_type=jnp.float32
        )
        observed = block_ref[:, step * width : (step + 1) * width].astype(jnp.float32)
        resid = (0.5 * jnp.tanh(model) + (0.5 - observed)).astype(jnp.bfloat16)
        total = total + jnp.dot(resid, pair, preferred_element_type=jnp.float32)
    return total


def block_kernel(
    local_blocks, coords_ref, owner_ref, count_ref, blocks_ref, table_ref, parts_ref, slot_ref,
    block_buf, rows_buf, part_buf, sems, part_sems,
):
    slots, edge, _ = blocks_ref.shape
    depth = block_buf.shape[0]
    modes = rows_buf.shape[1]
    count = count_ref[0]

    def copies(s):
        at = lax.rem(s, depth)
        made = [pltpu.make_async_copy(blocks_ref.at[s], block_buf.at[at], sems.at[at, modes])]
        for m in range(modes):
            pos = owner_ref[m, coords_ref[m, s]]
            row = (lax.div(pos, local_blocks) * modes + m) * local_blocks + lax.rem(pos, local_blocks)
            made.append(
                pltpu.make_async_copy(table_ref.at[row], rows_buf.at[at, m], sems.at[at, m])
            )
        return made

    def fetch(s):
        @pl.when(s < count)
        def _():
            for copy in copies(s):
                copy.start()

    for s in range(depth - 2):
        fetch(s)

    @pl.loop(0, slot_ref.shape[0])
    def _(p):
        slot_ref[p] = slots

    @pl.loop(0, count)
    def _(s):
        slot_ref[owner_ref[0, coords_ref[0, s]]] = s

    def store(s):
        return pltpu.make_async_copy(part_buf.at[s], parts_ref.at[s], part_sems.at[s])

    part_buf[slots] = jnp.zeros(part_buf.shape[1:], jnp.float32)
    store(slots).start()

    def compute(s):
        at = lax.rem(s, depth)
        half_a = rows_buf[at, 0] * jnp.bfloat16(0.5)
        part_buf[s] = block_part(
            edge, 16, half_a, rows_buf.at[at, 1], rows_buf[at, 2], block_buf.at[at]
        )
        store(s).start()

    pairs = lax.div(count, 2)

    @pl.loop(0, pairs)
    def _(h):
        for q in range(2):
            fetch(2 * h + depth - 2 + q)
        for q in range(2):
            for copy in copies(2 * h + q):
                copy.wait()
        for q in range(2):
            compute(2 * h + q)

    @pl.when(2 * pairs < count)
    def _():
        for copy in copies(2 * pairs):
            copy.wait()
        compute(2 * pairs)

    @pl.loop(0, count)
    def _(s):
        store(s).wait()

    store(slots).wait()


def block_gradients(tensor_blocks, table, coords, owner, count, positions, local_blocks):
    slots, edge, merged = tensor_blocks.shape
    modes, _ = coords.shape
    rank = table.shape[2]
    depth = 6
    smem = pl.BlockSpec(memory_space=pltpu.SMEM)
    far = pl.BlockSpec(memory_space=pltpu.HBM)
    return pl.pallas_call(
        functools.partial(block_kernel, local_blocks),
        out_shape=(
            jax.ShapeDtypeStruct((slots + 1, edge, rank), jnp.float32),
            jax.ShapeDtypeStruct((positions,), jnp.int32),
        ),
        in_specs=[smem, smem, smem, far, far],
        out_specs=(far, smem),
        scratch_shapes=[
            pltpu.VMEM((depth, edge, merged), jnp.bfloat16),
            pltpu.VMEM((depth, modes, edge, rank), jnp.bfloat16),
            pltpu.VMEM((slots + 1, edge, rank), jnp.float32),
            pltpu.SemaphoreType.DMA((depth, modes + 1)),
            pltpu.SemaphoreType.DMA((slots + 1,)),
        ],
        compiler_params=pltpu.CompilerParams(vmem_limit_bytes=62 << 20),
        cost_estimate=pl.CostEstimate(
            flops=4 * slots * edge * merged * rank,
            bytes_accessed=2 * slots * edge * (merged + 5 * rank),
            transcendentals=slots * edge * merged,
        ),
    )(coords, owner, count, tensor_blocks, table)


CUTS = (((0, 88), (0, 128)), ((0, 88), (128, 256)), ((88, 128), (0, 256)))
SPLITS = ((48, 40), (48, 40), (24, 16))


def half_shape(part, stage):
    (r0, r1), (c0, c1) = CUTS[part]
    sizes = [RING, RING, RING]
    for axis in ORDERS[part][: stage + 1]:
        sizes[axis] = None
    if stage < 2:
        sizes[ORDERS[part][stage + 1]] = 2
        rows = r1 - r0
    else:
        rows = SPLITS[part][0]
    return tuple(n for n in sizes if n is not None) + (rows, c1 - c0)


def scatter_kernel(slot_ref, parts_ref, grad_ref, acc, outbox, inbox, *rest):
    buffers = rest[:9]
    send, recv, pair_send, pair_recv = rest[9:]
    place = Place()
    edge = parts_ref.shape[1]

    def region(ref, part, stage, k, half):
        order = ORDERS[part]
        (r0, r1), (c0, c1) = CUTS[part]
        index = [slice(None)] * 3
        for axis in order[:stage]:
            index[axis] = 0
        index[order[stage]] = k
        if half is not None:
            if stage < 2:
                index[order[stage + 1]] = slice(2 * half, 2 * half + 2)
            else:
                cut = r0 + SPLITS[part][0]
                r0, r1 = (r0, cut) if half == 0 else (cut, r1)
        return ref.at[index[0], index[1], index[2], r0:r1, c0:c1]

    def half_of(way, k):
        return way if k != 1 else 1 - way

    def landing(part, stage, way, k):
        ref = buffers[part * 3 + stage].at[way, k]
        if stage == 2:
            ref = ref.at[0 : SPLITS[part][half_of(way, k)]]
        return ref

    def outgoing(part, stage, way, k):
        offset = 2 if k == 0 else (3 if way == 0 else 1)
        src = region(acc, part, stage, offset, half_of(way, k))
        device = place.neighbour(ORDERS[part][stage], -1 if way == 0 else 1)
        at = (part, stage, way, k)
        return remote(src, landing(part, stage, way, k), send.at[at], recv.at[at], device)

    def take(part, stage, way, k):
        outgoing(part, stage, way, k).wait_recv()
        offset = (3 if way == 0 else 1) if k == 0 else 0
        target = region(acc, part, stage, offset, half_of(way, k))
        target[...] = target[...] + landing(part, stage, way, k)[...]

    def across(part, k):
        at = (part, k)
        return remote(
            region(outbox, part, 0, k, None),
            region(inbox, part, 0, k, None),
            pair_send.at[at],
            pair_recv.at[at],
            place.partner(),
        )

    def take_across(part, k):
        across(part, k).wait_recv()
        target = region(acc, part, 0, k, None)
        target[...] = target[...] + region(inbox, part, 0, k, None)[...]

    def spread(ref, core):
        @pl.loop(0, RING**3)
        def _(r):
            step = (lax.div(r, 16), lax.rem(lax.div(r, 4), 4), lax.rem(r, 4))
            blk, grp = place.device(
                [lax.rem(v + s, RING) for v, s in zip(place.coord, step)], core
            )
            first = (blk * 4 + grp) * 2
            for j in range(2):
                ref[step[0], step[1], step[2], j * edge : (j + 1) * edge, :] = parts_ref[
                    slot_ref[first + j]
                ]

    spread(outbox, 1 - place.core)
    place.greet()
    for k in (2, 3, 1, 0):
        for part in range(3):
            across(part, k).start()
    spread(acc, place.core)
    for part in range(3):
        take_across(part, 2)
        for way in range(2):
            outgoing(part, 0, way, 0).start()
    for part in range(3):
        for way, k in ((0, 3), (1, 1)):
            take_across(part, k)
            outgoing(part, 0, way, 1).start()
    for stage in range(3):
        for part in range(3):
            for way in range(2):
                take(part, stage, way, 0)
                outgoing(part, stage, way, 2).start()
        if stage == 0:
            for part in range(3):
                take_across(part, 0)
        for part in range(3):
            for k in (1, 2):
                for way in range(2):
                    take(part, stage, way, k)
            if stage < 2:
                for k in range(2):
                    for way in range(2):
                        outgoing(part, stage + 1, way, k).start()
    grad_ref[...] = acc[0, 0, 0]
    for part in range(3):
        for k in range(4):
            across(part, k).wait_send()
        for stage in range(3):
            for way in range(2):
                for k in range(3):
                    outgoing(part, stage, way, k).wait_send()


def scatter_gradients(parts, slot_of):
    edge, rank = parts.shape[1:]
    dense = (RING, RING, RING, 2 * edge, rank)
    buffers = [
        pltpu.VMEM((2, 3) + half_shape(part, stage), jnp.float32)
        for part in range(3)
        for stage in range(3)
    ]
    return pl.pallas_call(
        scatter_kernel,
        out_shape=jax.ShapeDtypeStruct((2 * edge, rank), jnp.float32),
        in_specs=[
            pl.BlockSpec(memory_space=pltpu.SMEM),
            pl.BlockSpec(memory_space=pltpu.VMEM),
        ],
        out_specs=pl.BlockSpec(memory_space=pltpu.VMEM),
        scratch_shapes=[pltpu.VMEM(dense, jnp.float32)] * 3
        + buffers
        + [
            pltpu.SemaphoreType.DMA((3, 3, 2, 3)),
            pltpu.SemaphoreType.DMA((3, 3, 2, 3)),
            pltpu.SemaphoreType.DMA((3, 4)),
            pltpu.SemaphoreType.DMA((3, 4)),
        ],
        compiler_params=pltpu.CompilerParams(
            collective_id=1, has_side_effects=True, vmem_limit_bytes=62 << 20
        ),
    )(slot_of, parts)


def per_device(tensor_blocks, block_coords, block_count, row_owner, factors, moment1, moment2):
    edge = tensor_blocks.shape[1]
    modes, local_rows, rank = factors.shape
    local_blocks = local_rows // edge
    positions = lax.axis_size(AXES) * local_blocks
    table = gather_rows(factors).reshape(modes * positions, edge, rank)
    parts, slot_of = block_gradients(
        tensor_blocks, table, block_coords, row_owner, block_count, positions, local_blocks
    )
    grad = scatter_gradients(parts, slot_of)
    new_moment1 = 0.9 * moment1 + 0.1 * grad
    new_moment2 = 0.999 * moment2 + 0.001 * grad * grad
    new_factor = factors[0] - 0.02 * (new_moment1 / (1.0 - 0.9**8)) / (
        jnp.sqrt(new_moment2 / (1.0 - 0.999**8)) + 1e-08
    )
    return (new_factor, new_moment1, new_moment2)


def solution(mesh):
    return jax.shard_map(
        per_device,
        mesh=mesh,
        in_specs=(
            P(AXES, None, None),
            P(None, AXES),
            P(AXES),
            P(),
            P(None, AXES, None),
            P(AXES, None),
            P(AXES, None),
        ),
        out_specs=(P(AXES, None), P(AXES, None), P(AXES, None)),
        check_vma=False,
    )
```

```python
import functools

import jax
import jax.numpy as jnp
from jax import lax
from jax.experimental import pallas as pl
from jax.experimental.pallas import tpu as pltpu
from jax.sharding import PartitionSpec as P

AXES = ("blk", "grp")
MESH = pl.DeviceIdType.MESH
RING = 4
ORDERS = ((0, 1, 2), (1, 2, 0), (2, 0, 1))


class Place:
    def __init__(self):
        blk = lax.axis_index("blk")
        self.coord = [lax.div(blk, 8), lax.rem(lax.div(blk, 2), 4), lax.axis_index("grp")]
        self.core = lax.rem(blk, 2)

    @staticmethod
    def device(coord, core):
        return (coord[0] * 8 + coord[1] * 2 + core, coord[2])

    def partner(self):
        return self.device(self.coord, 1 - self.core)

    def along(self, axis, step):
        return lax.rem(self.coord[axis] + (RING + step), RING)

    def neighbour(self, axis, step):
        coord = list(self.coord)
        coord[axis] = self.along(axis, step)
        return self.device(coord, self.core)

    def offset(self, device):
        blk = lax.div(device, RING)
        coord = (lax.div(blk, 8), lax.rem(lax.div(blk, 2), 4), lax.rem(device, RING))
        steps = [lax.rem(v - me + RING, RING) for v, me in zip(coord, self.coord)]
        side = lax.rem(lax.rem(blk, 2) + self.core, 2)
        return ((steps[0] * RING + steps[1]) * RING + steps[2]) * 2 + side

    def greet(self):
        barrier = pltpu.get_barrier_semaphore()
        peers = [self.neighbour(axis, step) for axis in range(3) for step in (1, -1)]
        for peer in peers + [self.partner()]:
            pl.semaphore_signal(barrier, inc=1, device_id=peer, device_id_type=MESH)
        pl.semaphore_wait(barrier, 7)


def remote(src, dst, send, recv, device):
    return pltpu.make_async_remote_copy(
        src_ref=src, dst_ref=dst, send_sem=send, recv_sem=recv, device_id=device, device_id_type=MESH
    )


ALL = slice(0, RING)
FAR = slice(1, RING)
GROUPS = (
    ((),),
    ((0,), (FAR,)),
    ((0, 0), (FAR, 0), (ALL, 1), (ALL, 3), (ALL, 2)),
)
LISTED = [(stage, g) for stage in range(3) for g in range(len(GROUPS[stage]))]
NUMBER = {at: i for i, at in enumerate(LISTED)}


def gather_kernel(own_ref, table_ref, cast_ref, local_sem, own_sem, send, recv, pair_send, pair_recv):
    place = Place()
    half_rows = cast_ref.shape[1] // 2

    def region(part, stage, g, value, half, side):
        index = [0, 0, 0]
        for axis, piece in zip(ORDERS[part], GROUPS[stage][g]):
            index[axis] = piece
        index[ORDERS[part][stage]] = value
        rows = slice(0, 2 * half_rows) if half is None else slice(half * half_rows, (half + 1) * half_rows)
        return table_ref.at[index[0], index[1], index[2], side, part, rows]

    def half_of(way, k):
        return way if k != 1 else 1 - way

    def copy(part, stage, g, way, k):
        half = half_of(way, k)
        came = 3 if way == 0 else 1
        if k == 2:
            src = region(part, stage, g, came, half, 0)
            dst = region(part, stage, g, 2, half, 0)
        else:
            src = region(part, stage, g, 0, half, 0)
            dst = region(part, stage, g, came, half, 0)
            if g == 0:
                src = cast_ref.at[part, half * half_rows : (half + 1) * half_rows]
        device = place.neighbour(ORDERS[part][stage], 1 if way == 0 else -1)
        at = (part, NUMBER[stage, g], way, k)
        return remote(src, dst, send.at[at], recv.at[at], device)

    def across(part, stage, g, way, j):
        value, half = ((3 if way == 0 else 1), None) if j == 0 else (2, way)
        at = (part, NUMBER[stage, g], way, j)
        return remote(
            region(part, stage, g, value, half, 0),
            region(part, stage, g, value, half, 1),
            pair_send.at[at],
            pair_recv.at[at],
            place.partner(),
        )

    steps = [(part, way) for part in range(3) for way in range(2)]

    def begin(stage, g):
        for k in range(2):
            for part, way in steps:
                copy(part, stage, g, way, k).start()

    def arrive(stage, g, k):
        for part, way in steps:
            copy(part, stage, g, way, k).wait_recv()
            if k == 0:
                copy(part, stage, g, way, 2).start()
            else:
                across(part, stage, g, way, k - 1).start()

    def drain(stage, g):
        for part, way in steps:
            for k in range(3):
                copy(part, stage, g, way, k).wait_send()
            for j in range(2):
                across(part, stage, g, way, j).wait_send()

    def collect(stage, g):
        for part, way in steps:
            for j in range(2):
                across(part, stage, g, way, j).wait_recv()

    cast_ref[...] = own_ref[...].astype(cast_ref.dtype)
    place.greet()
    for stage in range(3):
        begin(stage, 0)
    mine = pltpu.make_async_copy(cast_ref, table_ref.at[0, 0, 0, 0], local_sem)
    mine.start()
    own = remote(cast_ref, table_ref.at[0, 0, 0, 1], own_sem.at[0], own_sem.at[1], place.partner())
    own.start()
    mine.wait()
    arrive(0, 0, 0)
    arrive(0, 0, 1)
    arrive(1, 0, 0)
    arrive(0, 0, 2)
    begin(1, 1)
    begin(2, 1)
    arrive(2, 0, 0)
    for k in range(1, 3):
        arrive(1, 0, k)
        arrive(2, 0, k)
    arrive(1, 1, 0)
    arrive(1, 1, 1)
    begin(2, 2)
    begin(2, 3)
    arrive(2, 1, 0)
    arrive(1, 1, 2)
    begin(2, 4)
    arrive(2, 1, 1)
    arrive(2, 1, 2)
    own.wait()
    for at in ((0, 0), (1, 0), (2, 0), (1, 1)):
        drain(*at)
        collect(*at)
    for g in (2, 3, 4):
        arrive(2, g, 0)
        arrive(2, g, 1)
    drain(2, 1)
    collect(2, 1)
    for g in (2, 3, 4):
        arrive(2, g, 2)
    for g in (2, 3, 4):
        drain(2, g)
        collect(2, g)


def gather_rows(factors):
    modes, rows, rank = factors.shape
    count = len(LISTED)
    return pl.pallas_call(
        gather_kernel,
        out_shape=jax.ShapeDtypeStruct((RING, RING, RING, 2, modes, rows, rank), jnp.bfloat16),
        in_specs=[pl.BlockSpec(memory_space=pltpu.VMEM)],
        out_specs=pl.BlockSpec(memory_space=pl.ANY),
        scratch_shapes=[
            pltpu.VMEM((modes, rows, rank), jnp.bfloat16),
            pltpu.SemaphoreType.DMA,
            pltpu.SemaphoreType.DMA((2,)),
            pltpu.SemaphoreType.DMA((3, count, 2, 3)),
            pltpu.SemaphoreType.DMA((3, count, 2, 3)),
            pltpu.SemaphoreType.DMA((3, count, 2, 2)),
            pltpu.SemaphoreType.DMA((3, count, 2, 2)),
        ],
        compiler_params=pltpu.CompilerParams(collective_id=0, has_side_effects=True),
    )(factors)


def block_part(edge, chunk, half_a, b_ref, rows_c, block_ref):
    total = jnp.zeros((edge, rows_c.shape[1]), jnp.float32)
    width = chunk * edge
    for step in range(edge // chunk):
        pair = jnp.concatenate(
            [b_ref[pl.ds(step * chunk + j, 1), :] * rows_c for j in range(chunk)], axis=0
        )
        model = lax.dot_general(
            half_a, pair, (((1,), (1,)), ((), ())), preferred_element_type=jnp.float32
        )
        observed = block_ref[:, step * width : (step + 1) * width].astype(jnp.float32)
        resid = (0.5 * jnp.tanh(model) + (0.5 - observed)).astype(jnp.bfloat16)
        total = total + jnp.dot(resid, pair, preferred_element_type=jnp.float32)
    return total


def block_kernel(
    local_blocks, coords_ref, owner_ref, count_ref, blocks_ref, table_ref, parts_ref, slot_ref,
    block_buf, rows_buf, part_buf, sems, part_sems,
):
    slots, edge, _ = blocks_ref.shape
    depth = block_buf.shape[0]
    modes = rows_buf.shape[1]
    count = count_ref[0]
    place = Place()

    def copies(s):
        at = lax.rem(s, depth)
        made = [pltpu.make_async_copy(blocks_ref.at[s], block_buf.at[at], sems.at[at, modes])]
        for m in range(modes):
            pos = owner_ref[m, coords_ref[m, s]]
            row = (place.offset(lax.div(pos, local_blocks)) * modes + m) * local_blocks
            row = row + lax.rem(pos, local_blocks)
            made.append(
                pltpu.make_async_copy(table_ref.at[row], rows_buf.at[at, m], sems.at[at, m])
            )
        return made

    def fetch(s):
        @pl.when(s < count)
        def _():
            for copy in copies(s):
                copy.start()

    for s in range(depth - 2):
        fetch(s)

    @pl.loop(0, slot_ref.shape[0])
    def _(p):
        slot_ref[p] = slots

    @pl.loop(0, count)
    def _(s):
        slot_ref[owner_ref[0, coords_ref[0, s]]] = s

    def store(s):
        return pltpu.make_async_copy(part_buf.at[s], parts_ref.at[s], part_sems.at[s])

    part_buf[slots] = jnp.zeros(part_buf.shape[1:], jnp.float32)
    store(slots).start()

    def compute(s):
        at = lax.rem(s, depth)
        half_a = rows_buf[at, 0] * jnp.bfloat16(0.5)
        part_buf[s] = block_part(
            edge, 16, half_a, rows_buf.at[at, 1], rows_buf[at, 2], block_buf.at[at]
        )
        store(s).start()

    pairs = lax.div(count, 2)

    @pl.loop(0, pairs)
    def _(h):
        for q in range(2):
            fetch(2 * h + depth - 2 + q)
        for q in range(2):
            for copy in copies(2 * h + q):
                copy.wait()
        for q in range(2):
            compute(2 * h + q)

    @pl.when(2 * pairs < count)
    def _():
        for copy in copies(2 * pairs):
            copy.wait()
        compute(2 * pairs)

    @pl.loop(0, count)
    def _(s):
        store(s).wait()

    store(slots).wait()


def block_gradients(tensor_blocks, table, coords, owner, count, positions, local_blocks):
    slots, edge, merged = tensor_blocks.shape
    modes, _ = coords.shape
    rank = table.shape[2]
    depth = 6
    smem = pl.BlockSpec(memory_space=pltpu.SMEM)
    far = pl.BlockSpec(memory_space=pltpu.HBM)
    return pl.pallas_call(
        functools.partial(block_kernel, local_blocks),
        out_shape=(
            jax.ShapeDtypeStruct((slots + 1, edge, rank), jnp.float32),
            jax.ShapeDtypeStruct((positions,), jnp.int32),
        ),
        in_specs=[smem, smem, smem, far, far],
        out_specs=(far, smem),
        scratch_shapes=[
            pltpu.VMEM((depth, edge, merged), jnp.bfloat16),
            pltpu.VMEM((depth, modes, edge, rank), jnp.bfloat16),
            pltpu.VMEM((slots + 1, edge, rank), jnp.float32),
            pltpu.SemaphoreType.DMA((depth, modes + 1)),
            pltpu.SemaphoreType.DMA((slots + 1,)),
        ],
        compiler_params=pltpu.CompilerParams(vmem_limit_bytes=62 << 20),
        cost_estimate=pl.CostEstimate(
            flops=4 * slots * edge * merged * rank,
            bytes_accessed=2 * slots * edge * (merged + 5 * rank),
            transcendentals=slots * edge * merged,
        ),
    )(coords, owner, count, tensor_blocks, table)


CUTS = (((0, 88), (0, 128)), ((0, 88), (128, 256)), ((88, 128), (0, 256)))
SPLITS = ((48, 40), (48, 40), (24, 16))


def half_shape(part, stage):
    (r0, r1), (c0, c1) = CUTS[part]
    sizes = [RING, RING, RING]
    for axis in ORDERS[part][: stage + 1]:
        sizes[axis] = None
    if stage < 2:
        sizes[ORDERS[part][stage + 1]] = 2
        rows = r1 - r0
    else:
        rows = SPLITS[part][0]
    return tuple(n for n in sizes if n is not None) + (rows, c1 - c0)


def scatter_kernel(slot_ref, parts_ref, grad_ref, acc, outbox, inbox, *rest):
    buffers = rest[:9]
    send, recv, pair_send, pair_recv = rest[9:]
    place = Place()
    edge = parts_ref.shape[1]

    def region(ref, part, stage, k, half):
        order = ORDERS[part]
        (r0, r1), (c0, c1) = CUTS[part]
        index = [slice(None)] * 3
        for axis in order[:stage]:
            index[axis] = 0
        index[order[stage]] = k
        if half is not None:
            if stage < 2:
                index[order[stage + 1]] = slice(2 * half, 2 * half + 2)
            else:
                cut = r0 + SPLITS[part][0]
                r0, r1 = (r0, cut) if half == 0 else (cut, r1)
        return ref.at[index[0], index[1], index[2], r0:r1, c0:c1]

    def half_of(way, k):
        return way if k != 1 else 1 - way

    def landing(part, stage, way, k):
        ref = buffers[part * 3 + stage].at[way, k]
        if stage == 2:
            ref = ref.at[0 : SPLITS[part][half_of(way, k)]]
        return ref

    def outgoing(part, stage, way, k):
        offset = 2 if k == 0 else (3 if way == 0 else 1)
        src = region(acc, part, stage, offset, half_of(way, k))
        device = place.neighbour(ORDERS[part][stage], -1 if way == 0 else 1)
        at = (part, stage, way, k)
        return remote(src, landing(part, stage, way, k), send.at[at], recv.at[at], device)

    def take(part, stage, way, k):
        outgoing(part, stage, way, k).wait_recv()
        offset = (3 if way == 0 else 1) if k == 0 else 0
        target = region(acc, part, stage, offset, half_of(way, k))
        target[...] = target[...] + landing(part, stage, way, k)[...]

    def across(part, k):
        at = (part, k)
        return remote(
            region(outbox, part, 0, k, None),
            region(inbox, part, 0, k, None),
            pair_send.at[at],
            pair_recv.at[at],
            place.partner(),
        )

    def take_across(part, k):
        across(part, k).wait_recv()
        target = region(acc, part, 0, k, None)
        target[...] = target[...] + region(inbox, part, 0, k, None)[...]

    def spread(ref, core):
        @pl.loop(0, RING**3)
        def _(r):
            step = (lax.div(r, 16), lax.rem(lax.div(r, 4), 4), lax.rem(r, 4))
            blk, grp = place.device(
                [lax.rem(v + s, RING) for v, s in zip(place.coord, step)], core
            )
            first = (blk * 4 + grp) * 2
            for j in range(2):
                ref[step[0], step[1], step[2], j * edge : (j + 1) * edge, :] = parts_ref[
                    slot_ref[first + j]
                ]

    spread(outbox, 1 - place.core)
    place.greet()
    for k in (2, 3, 1, 0):
        for part in range(3):
            across(part, k).start()
    spread(acc, place.core)
    for part in range(3):
        take_across(part, 2)
        for way in range(2):
            outgoing(part, 0, way, 0).start()
    for part in range(3):
        for way, k in ((0, 3), (1, 1)):
            take_across(part, k)
            outgoing(part, 0, way, 1).start()
    for stage in range(3):
        for part in range(3):
            for way in range(2):
                take(part, stage, way, 0)
                outgoing(part, stage, way, 2).start()
        if stage == 0:
            for part in range(3):
                take_across(part, 0)
        for part in range(3):
            for k in (1, 2):
                for way in range(2):
                    take(part, stage, way, k)
            if stage < 2:
                for k in range(2):
                    for way in range(2):
                        outgoing(part, stage + 1, way, k).start()
    grad_ref[...] = acc[0, 0, 0]
    for part in range(3):
        for k in range(4):
            across(part, k).wait_send()
        for stage in range(3):
            for way in range(2):
                for k in range(3):
                    outgoing(part, stage, way, k).wait_send()


def scatter_gradients(parts, slot_of):
    edge, rank = parts.shape[1:]
    dense = (RING, RING, RING, 2 * edge, rank)
    buffers = [
        pltpu.VMEM((2, 3) + half_shape(part, stage), jnp.float32)
        for part in range(3)
        for stage in range(3)
    ]
    return pl.pallas_call(
        scatter_kernel,
        out_shape=jax.ShapeDtypeStruct((2 * edge, rank), jnp.float32),
        in_specs=[
            pl.BlockSpec(memory_space=pltpu.SMEM),
            pl.BlockSpec(memory_space=pltpu.VMEM),
        ],
        out_specs=pl.BlockSpec(memory_space=pltpu.VMEM),
        scratch_shapes=[pltpu.VMEM(dense, jnp.float32)] * 3
        + buffers
        + [
            pltpu.SemaphoreType.DMA((3, 3, 2, 3)),
            pltpu.SemaphoreType.DMA((3, 3, 2, 3)),
            pltpu.SemaphoreType.DMA((3, 4)),
            pltpu.SemaphoreType.DMA((3, 4)),
        ],
        compiler_params=pltpu.CompilerParams(
            collective_id=1, has_side_effects=True, vmem_limit_bytes=62 << 20
        ),
    )(slot_of, parts)


def per_device(tensor_blocks, block_coords, block_count, row_owner, factors, moment1, moment2):
    edge = tensor_blocks.shape[1]
    modes, local_rows, rank = factors.shape
    local_blocks = local_rows // edge
    positions = lax.axis_size(AXES) * local_blocks
    table = gather_rows(factors).reshape(modes * positions, edge, rank)
    parts, slot_of = block_gradients(
        tensor_blocks, table, block_coords, row_owner, block_count, positions, local_blocks
    )
    grad = scatter_gradients(parts, slot_of)
    new_moment1 = 0.9 * moment1 + 0.1 * grad
    new_moment2 = 0.999 * moment2 + 0.001 * grad * grad
    new_factor = factors[0] - 0.02 * (new_moment1 / (1.0 - 0.9**8)) / (
        jnp.sqrt(new_moment2 / (1.0 - 0.999**8)) + 1e-08
    )
    return (new_factor, new_moment1, new_moment2)


def solution(mesh):
    return jax.shard_map(
        per_device,
        mesh=mesh,
        in_specs=(
            P(AXES, None, None),
            P(None, AXES),
            P(AXES),
            P(),
            P(None, AXES, None),
            P(AXES, None),
            P(AXES, None),
        ),
        out_specs=(P(AXES, None), P(AXES, None), P(AXES, None)),
        check_vma=False,
    )
```

```python
import functools

import jax
import jax.numpy as jnp
from jax import lax
from jax.experimental import pallas as pl
from jax.experimental.pallas import tpu as pltpu
from jax.sharding import PartitionSpec as P

AXES = ("blk", "grp")
MESH = pl.DeviceIdType.MESH
RING = 4
ORDERS = ((0, 1, 2), (1, 2, 0), (2, 0, 1))


class Place:
    def __init__(self):
        blk = lax.axis_index("blk")
        self.coord = [lax.div(blk, 8), lax.rem(lax.div(blk, 2), 4), lax.axis_index("grp")]
        self.core = lax.rem(blk, 2)

    @staticmethod
    def device(coord, core):
        return (coord[0] * 8 + coord[1] * 2 + core, coord[2])

    def partner(self):
        return self.device(self.coord, 1 - self.core)

    def along(self, axis, step):
        return lax.rem(self.coord[axis] + (RING + step), RING)

    def neighbour(self, axis, step):
        coord = list(self.coord)
        coord[axis] = self.along(axis, step)
        return self.device(coord, self.core)

    def greet(self):
        self.announce()
        self.await_peers()

    def announce(self):
        barrier = pltpu.get_barrier_semaphore()
        peers = [self.neighbour(axis, step) for axis in range(3) for step in (1, -1)]
        for peer in peers + [self.partner()]:
            pl.semaphore_signal(barrier, inc=1, device_id=peer, device_id_type=MESH)

    def await_peers(self):
        pl.semaphore_wait(pltpu.get_barrier_semaphore(), 7)


def remote(src, dst, send, recv, device):
    return pltpu.make_async_remote_copy(
        src_ref=src, dst_ref=dst, send_sem=send, recv_sem=recv, device_id=device, device_id_type=MESH
    )


def gather_kernel(own_ref, table_ref, cast_ref, local_sem, own_sem, send, recv, pair_send, pair_recv):
    place = Place()
    x, y, z = place.coord
    core = place.core
    other = 1 - core
    half_rows = cast_ref.shape[1] // 2

    def region(part, stage, value, half, side):
        index = list(place.coord)
        for axis in ORDERS[part][:stage]:
            index[axis] = slice(None)
        index[ORDERS[part][stage]] = value
        return table_ref.at[
            index[0], index[1], side, index[2], part, half * half_rows : (half + 1) * half_rows
        ]

    def arrived(part, stage, way, k, side):
        axis = ORDERS[part][stage]
        step = -1 if way == 0 else 1
        value = place.along(axis, step if k < 2 else 2)
        return region(part, stage, value, way if k != 1 else 1 - way, side)

    def outgoing(part, stage, way, k):
        axis = ORDERS[part][stage]
        half = way if k != 1 else 1 - way
        if k < 2:
            dst = region(part, stage, place.coord[axis], half, core)
            src = dst
            if stage == 0:
                src = cast_ref.at[part, half * half_rows : (half + 1) * half_rows]
        else:
            dst = src = arrived(part, stage, way, 0, core)
        device = place.neighbour(axis, 1 if way == 0 else -1)
        return remote(src, dst, send.at[part, stage, way, k], recv.at[part, stage, way, k], device)

    def incoming(part, stage, way, k):
        ref = arrived(part, stage, way, k, core)
        axis = ORDERS[part][stage]
        device = place.neighbour(axis, 1 if way == 0 else -1)
        return remote(ref, ref, send.at[part, stage, way, k], recv.at[part, stage, way, k], device)

    def across(part, stage, way, k, side):
        ref = arrived(part, stage, way, k, side)
        at = (part, stage, way, k)
        return remote(ref, ref, pair_send.at[at], pair_recv.at[at], place.partner())

    cast_ref[...] = own_ref[...].astype(cast_ref.dtype)
    place.greet()
    steps = [(part, way) for part in range(3) for way in range(2)]
    for k in range(2):
        for part, way in steps:
            outgoing(part, 0, way, k).start()
    mine = pltpu.make_async_copy(cast_ref, table_ref.at[x, y, core, z], local_sem)
    mine.start()
    own = remote(cast_ref, table_ref.at[x, y, core, z], own_sem.at[0], own_sem.at[1], place.partner())
    own.start()
    mine.wait()
    for stage in range(3):
        for k in range(3):
            for part in range(3):
                for way in range(2):
                    incoming(part, stage, way, k).wait_recv()
                    if k == 0:
                        outgoing(part, stage, way, 2).start()
                    across(part, stage, way, k, core).start()
                if k == 2 and stage < 2:
                    for way in range(2):
                        outgoing(part, stage + 1, way, 0).start()
                        outgoing(part, stage + 1, way, 1).start()
    own.wait_send()
    theirs = table_ref.at[x, y, other, z]
    remote(theirs, theirs, own_sem.at[0], own_sem.at[1], place.partner()).wait_recv()
    for stage in range(3):
        for k in range(3):
            for part, way in steps:
                outgoing(part, stage, way, k).wait_send()
                across(part, stage, way, k, core).wait_send()
                across(part, stage, way, k, other).wait_recv()


def gather_rows(factors):
    modes, rows, rank = factors.shape
    return pl.pallas_call(
        gather_kernel,
        out_shape=jax.ShapeDtypeStruct((4, 4, 2, 4, modes, rows, rank), jnp.bfloat16),
        in_specs=[pl.BlockSpec(memory_space=pltpu.VMEM)],
        out_specs=pl.BlockSpec(memory_space=pl.ANY),
        scratch_shapes=[
            pltpu.VMEM((modes, rows, rank), jnp.bfloat16),
            pltpu.SemaphoreType.DMA,
            pltpu.SemaphoreType.DMA((2,)),
            pltpu.SemaphoreType.DMA((3, 3, 2, 3)),
            pltpu.SemaphoreType.DMA((3, 3, 2, 3)),
            pltpu.SemaphoreType.DMA((3, 3, 2, 3)),
            pltpu.SemaphoreType.DMA((3, 3, 2, 3)),
        ],
        compiler_params=pltpu.CompilerParams(collective_id=0, has_side_effects=True),
    )(factors)


def block_part(edge, chunk, half_a, b_ref, rows_c, block_ref):
    total = jnp.zeros((edge, rows_c.shape[1]), jnp.float32)
    width = chunk * edge
    for step in range(edge // chunk):
        pair = jnp.concatenate(
            [b_ref[pl.ds(step * chunk + j, 1), :] * rows_c for j in range(chunk)], axis=0
        )
        model = lax.dot_general(
            half_a, pair, (((1,), (1,)), ((), ())), preferred_element_type=jnp.float32
        )
        observed = block_ref[:, step * width : (step + 1) * width].astype(jnp.float32)
        resid = (0.5 * jnp.tanh(model) + (0.5 - observed)).astype(jnp.bfloat16)
        total = total + jnp.dot(resid, pair, preferred_element_type=jnp.float32)
    return total


def block_kernel(
    local_blocks, coords_ref, owner_ref, count_ref, blocks_ref, table_ref, parts_ref, slot_ref,
    block_buf, rows_buf, part_buf, sems, part_sems,
):
    slots, edge, _ = blocks_ref.shape
    depth = block_buf.shape[0]
    modes = rows_buf.shape[1]
    count = count_ref[0]

    def copies(s):
        at = lax.rem(s, depth)
        made = [pltpu.make_async_copy(blocks_ref.at[s], block_buf.at[at], sems.at[at, modes])]
        for m in range(modes):
            pos = owner_ref[m, coords_ref[m, s]]
            row = (lax.div(pos, local_blocks) * modes + m) * local_blocks + lax.rem(pos, local_blocks)
            made.append(
                pltpu.make_async_copy(table_ref.at[row], rows_buf.at[at, m], sems.at[at, m])
            )
        return made

    def fetch(s):
        @pl.when(s < count)
        def _():
            for copy in copies(s):
                copy.start()

    for s in range(depth - 2):
        fetch(s)

    @pl.loop(0, slot_ref.shape[0])
    def _(p):
        slot_ref[p] = slots

    @pl.loop(0, count)
    def _(s):
        slot_ref[owner_ref[0, coords_ref[0, s]]] = s

    def store(s):
        return pltpu.make_async_copy(part_buf.at[s], parts_ref.at[s], part_sems.at[s])

    part_buf[slots] = jnp.zeros(part_buf.shape[1:], jnp.float32)
    store(slots).start()

    def compute(s):
        at = lax.rem(s, depth)
        half_a = rows_buf[at, 0] * jnp.bfloat16(0.5)
        part_buf[s] = block_part(
            edge, 16, half_a, rows_buf.at[at, 1], rows_buf[at, 2], block_buf.at[at]
        )
        store(s).start()

    pairs = lax.div(count, 2)

    @pl.loop(0, pairs)
    def _(h):
        for q in range(2):
            fetch(2 * h + depth - 2 + q)
        for q in range(2):
            for copy in copies(2 * h + q):
                copy.wait()
        for q in range(2):
            compute(2 * h + q)

    @pl.when(2 * pairs < count)
    def _():
        for copy in copies(2 * pairs):
            copy.wait()
        compute(2 * pairs)

    @pl.loop(0, count)
    def _(s):
        store(s).wait()

    store(slots).wait()


def block_gradients(tensor_blocks, table, coords, owner, count, positions, local_blocks):
    slots, edge, merged = tensor_blocks.shape
    modes, _ = coords.shape
    rank = table.shape[2]
    depth = 6
    smem = pl.BlockSpec(memory_space=pltpu.SMEM)
    far = pl.BlockSpec(memory_space=pltpu.HBM)
    return pl.pallas_call(
        functools.partial(block_kernel, local_blocks),
        out_shape=(
            jax.ShapeDtypeStruct((slots + 1, edge, rank), jnp.float32),
            jax.ShapeDtypeStruct((positions,), jnp.int32),
        ),
        in_specs=[smem, smem, smem, far, far],
        out_specs=(far, smem),
        scratch_shapes=[
            pltpu.VMEM((depth, edge, merged), jnp.bfloat16),
            pltpu.VMEM((depth, modes, edge, rank), jnp.bfloat16),
            pltpu.VMEM((slots + 1, edge, rank), jnp.float32),
            pltpu.SemaphoreType.DMA((depth, modes + 1)),
            pltpu.SemaphoreType.DMA((slots + 1,)),
        ],
        compiler_params=pltpu.CompilerParams(vmem_limit_bytes=62 << 20),
        cost_estimate=pl.CostEstimate(
            flops=4 * slots * edge * merged * rank,
            bytes_accessed=2 * slots * edge * (merged + 5 * rank),
            transcendentals=slots * edge * merged,
        ),
    )(coords, owner, count, tensor_blocks, table)


CUTS = (((0, 88), (0, 128)), ((0, 88), (128, 256)), ((88, 128), (0, 256)))
SPLITS = ((48, 40), (48, 40), (24, 16))


def half_shape(part, stage):
    (r0, r1), (c0, c1) = CUTS[part]
    if stage == 2:
        return (SPLITS[part][0], c1 - c0)
    return ((8 if stage == 0 else 2) * (r1 - r0) + 16, c1 - c0)


def half_type(stage):
    return jnp.float32 if stage == 2 else jnp.int16


LEVELS = 32767.0


def scatter_kernel(slot_ref, parts_ref, grad_ref, acc, outbox, inbox, *rest):
    landed = rest[:9]
    packed = rest[9:15]
    send, recv, pair_send, pair_recv = rest[15:]
    place = Place()
    edge = parts_ref.shape[1]

    def spans(part, stage, k, half):
        order = ORDERS[part]
        (r0, r1), (c0, c1) = CUTS[part]
        index = [slice(0, RING)] * 3
        for axis in order[:stage]:
            index[axis] = 0
        index[order[stage]] = k
        if half is not None:
            if stage < 2:
                index[order[stage + 1]] = slice(2 * half, 2 * half + 2)
            else:
                cut = r0 + SPLITS[part][0]
                r0, r1 = (r0, cut) if half == 0 else (cut, r1)
        return index, slice(r0, r1), slice(c0, c1)

    def region(ref, part, stage, k, half):
        index, rows, cols = spans(part, stage, k, half)
        return ref.at[index[0], index[1], index[2], rows, cols]

    def cells(part, stage, k, half):
        index, rows, cols = spans(part, stage, k, half)
        each = [range(i.start, i.stop) if isinstance(i, slice) else (i,) for i in index]
        return [acc.at[x, y, z, rows, cols] for x in each[0] for y in each[1] for z in each[2]]

    def half_of(way, k):
        return way if k != 1 else 1 - way

    def landing(part, stage, way, k):
        ref = landed[part * 3 + stage].at[way, k]
        if stage == 2:
            ref = ref.at[0 : SPLITS[part][half_of(way, k)]]
        return ref

    def source(part, stage, way, k):
        if stage < 2:
            return packed[part * 2 + stage].at[way, k]
        return region(acc, part, stage, 2 if k == 0 else (3 if way == 0 else 1), half_of(way, k))

    def transfer(part, stage, way, k):
        device = place.neighbour(ORDERS[part][stage], -1 if way == 0 else 1)
        at = (part, stage, way, k)
        return remote(
            source(part, stage, way, k), landing(part, stage, way, k), send.at[at], recv.at[at], device
        )

    def emit(part, stage, way, k):
        if stage < 2:
            refs = cells(part, stage, 2 if k == 0 else (3 if way == 0 else 1), half_of(way, k))
            rows = refs[0].shape[0]
            peak = jnp.abs(refs[0][...])
            for ref in refs[1:]:
                peak = jnp.maximum(peak, jnp.abs(ref[...]))
            peak = jnp.maximum(jnp.max(peak, axis=0, keepdims=True), 1e-30)
            power = jnp.ceil(jnp.log2(peak))
            factor = jnp.exp2(-power) * LEVELS
            out = source(part, stage, way, k)
            for i in range(0, len(refs), 2):
                both = jnp.concatenate([refs[i][...], refs[i + 1][...]], axis=0)
                out[i * rows : (i + 2) * rows, :] = (
                    jnp.round(both * factor).astype(jnp.int32).astype(jnp.int16)
                )
            out[len(refs) * rows :, :] = jnp.broadcast_to(
                power, (16, power.shape[1])
            ).astype(jnp.int32).astype(jnp.int16)
        transfer(part, stage, way, k).start()

    def take(part, stage, way, k):
        transfer(part, stage, way, k).wait_recv()
        refs = cells(part, stage, (3 if way == 0 else 1) if k == 0 else 0, half_of(way, k))
        came = landing(part, stage, way, k)
        if stage == 2:
            refs[0][...] = refs[0][...] + came[...]
            return
        rows = refs[0].shape[0]
        power = came[len(refs) * rows :, :].astype(jnp.int32).astype(jnp.float32)[:1]
        factor = jnp.exp2(power) * (1.0 / LEVELS)
        for i in range(0, len(refs), 2):
            both = came[i * rows : (i + 2) * rows, :].astype(jnp.int32).astype(jnp.float32) * factor
            refs[i][...] = refs[i][...] + both[:rows]
            refs[i + 1][...] = refs[i + 1][...] + both[rows:]

    def across(part, k):
        at = (part, k)
        return remote(
            region(outbox, part, 0, k, None),
            region(inbox, part, 0, k, None),
            pair_send.at[at],
            pair_recv.at[at],
            place.partner(),
        )

    def take_across(part, k):
        across(part, k).wait_recv()
        target = region(acc, part, 0, k, None)
        target[...] = target[...] + region(inbox, part, 0, k, None)[...]

    def spread(ref, core):
        @pl.loop(0, RING**3)
        def _(r):
            step = (lax.div(r, 16), lax.rem(lax.div(r, 4), 4), lax.rem(r, 4))
            blk, grp = place.device(
                [lax.rem(v + s, RING) for v, s in zip(place.coord, step)], core
            )
            first = (blk * 4 + grp) * 2
            for j in range(2):
                ref[step[0], step[1], step[2], j * edge : (j + 1) * edge, :] = parts_ref[
                    slot_ref[first + j]
                ]

    place.announce()
    spread(outbox, 1 - place.core)
    place.await_peers()
    for k in (2, 3, 1, 0):
        for part in range(3):
            across(part, k).start()
    spread(acc, place.core)
    for part in range(3):
        take_across(part, 2)
        for way in range(2):
            emit(part, 0, way, 0)
    for part in range(3):
        for way, k in ((0, 3), (1, 1)):
            take_across(part, k)
            emit(part, 0, way, 1)
    for stage in range(3):
        for part in range(3):
            for way in range(2):
                take(part, stage, way, 0)
                emit(part, stage, way, 2)
        if stage == 0:
            for part in range(3):
                take_across(part, 0)
        for part in range(3):
            for k in (1, 2):
                for way in range(2):
                    take(part, stage, way, k)
            if stage < 2:
                for k in range(2):
                    for way in range(2):
                        emit(part, stage + 1, way, k)
    grad_ref[...] = acc[0, 0, 0]
    for part in range(3):
        for k in range(4):
            across(part, k).wait_send()
        for stage in range(3):
            for way in range(2):
                for k in range(3):
                    transfer(part, stage, way, k).wait_send()


def scatter_gradients(parts, slot_of):
    edge, rank = parts.shape[1:]
    dense = (RING, RING, RING, 2 * edge, rank)
    buffers = [
        pltpu.VMEM((2, 3) + half_shape(part, stage), half_type(stage))
        for stages in (range(3), range(2))
        for part in range(3)
        for stage in stages
    ]
    return pl.pallas_call(
        scatter_kernel,
        out_shape=jax.ShapeDtypeStruct((2 * edge, rank), jnp.float32),
        in_specs=[
            pl.BlockSpec(memory_space=pltpu.SMEM),
            pl.BlockSpec(memory_space=pltpu.VMEM),
        ],
        out_specs=pl.BlockSpec(memory_space=pltpu.VMEM),
        scratch_shapes=[pltpu.VMEM(dense, jnp.float32)] * 3
        + buffers
        + [
            pltpu.SemaphoreType.DMA((3, 3, 2, 3)),
            pltpu.SemaphoreType.DMA((3, 3, 2, 3)),
            pltpu.SemaphoreType.DMA((3, 4)),
            pltpu.SemaphoreType.DMA((3, 4)),
        ],
        compiler_params=pltpu.CompilerParams(
            collective_id=1, has_side_effects=True, vmem_limit_bytes=62 << 20
        ),
    )(slot_of, parts)


def per_device(tensor_blocks, block_coords, block_count, row_owner, factors, moment1, moment2):
    edge = tensor_blocks.shape[1]
    modes, local_rows, rank = factors.shape
    local_blocks = local_rows // edge
    positions = lax.axis_size(AXES) * local_blocks
    table = gather_rows(factors).reshape(modes * positions, edge, rank)
    parts, slot_of = block_gradients(
        tensor_blocks, table, block_coords, row_owner, block_count, positions, local_blocks
    )
    grad = scatter_gradients(parts, slot_of)
    new_moment1 = 0.9 * moment1 + 0.1 * grad
    new_moment2 = 0.999 * moment2 + 0.001 * grad * grad
    new_factor = factors[0] - 0.02 * (new_moment1 / (1.0 - 0.9**8)) / (
        jnp.sqrt(new_moment2 / (1.0 - 0.999**8)) + 1e-08
    )
    return (new_factor, new_moment1, new_moment2)


def solution(mesh):
    return jax.shard_map(
        per_device,
        mesh=mesh,
        in_specs=(
            P(AXES, None, None),
            P(None, AXES),
            P(AXES),
            P(),
            P(None, AXES, None),
            P(AXES, None),
            P(AXES, None),
        ),
        out_specs=(P(AXES, None), P(AXES, None), P(AXES, None)),
        check_vma=False,
    )
```

```python
import functools

import jax
import jax.numpy as jnp
from jax import lax
from jax.experimental import pallas as pl
from jax.experimental.pallas import tpu as pltpu
from jax.sharding import PartitionSpec as P

AXES = ("blk", "grp")
MESH = pl.DeviceIdType.MESH
RING = 4
ORDERS = ((0, 1, 2), (1, 2, 0), (2, 0, 1))


class Place:
    def __init__(self):
        blk = lax.axis_index("blk")
        self.coord = [lax.div(blk, 8), lax.rem(lax.div(blk, 2), 4), lax.axis_index("grp")]
        self.core = lax.rem(blk, 2)

    @staticmethod
    def device(coord, core):
        return (coord[0] * 8 + coord[1] * 2 + core, coord[2])

    def partner(self):
        return self.device(self.coord, 1 - self.core)

    def along(self, axis, step):
        return lax.rem(self.coord[axis] + (RING + step), RING)

    def neighbour(self, axis, step):
        coord = list(self.coord)
        coord[axis] = self.along(axis, step)
        return self.device(coord, self.core)

    def greet(self):
        self.announce()
        self.await_peers()

    def announce(self):
        barrier = pltpu.get_barrier_semaphore()
        peers = [self.neighbour(axis, step) for axis in range(3) for step in (1, -1)]
        for peer in peers + [self.partner()]:
            pl.semaphore_signal(barrier, inc=1, device_id=peer, device_id_type=MESH)

    def await_peers(self):
        pl.semaphore_wait(pltpu.get_barrier_semaphore(), 7)


def remote(src, dst, send, recv, device):
    return pltpu.make_async_remote_copy(
        src_ref=src, dst_ref=dst, send_sem=send, recv_sem=recv, device_id=device, device_id_type=MESH
    )


def gather_kernel(own_ref, table_ref, cast_ref, local_sem, own_sem, send, recv, pair_send, pair_recv):
    place = Place()
    x, y, z = place.coord
    core = place.core
    other = 1 - core
    half_rows = cast_ref.shape[1] // 2

    def region(part, stage, value, half, side):
        index = list(place.coord)
        for axis in ORDERS[part][:stage]:
            index[axis] = slice(None)
        index[ORDERS[part][stage]] = value
        return table_ref.at[
            index[0], index[1], side, index[2], part, half * half_rows : (half + 1) * half_rows
        ]

    def arrived(part, stage, way, k, side):
        axis = ORDERS[part][stage]
        step = -1 if way == 0 else 1
        value = place.along(axis, step if k < 2 else 2)
        return region(part, stage, value, way if k != 1 else 1 - way, side)

    def outgoing(part, stage, way, k):
        axis = ORDERS[part][stage]
        half = way if k != 1 else 1 - way
        if k < 2:
            dst = region(part, stage, place.coord[axis], half, core)
            src = dst
            if stage == 0:
                src = cast_ref.at[part, half * half_rows : (half + 1) * half_rows]
        else:
            dst = src = arrived(part, stage, way, 0, core)
        device = place.neighbour(axis, 1 if way == 0 else -1)
        return remote(src, dst, send.at[part, stage, way, k], recv.at[part, stage, way, k], device)

    def incoming(part, stage, way, k):
        ref = arrived(part, stage, way, k, core)
        axis = ORDERS[part][stage]
        device = place.neighbour(axis, 1 if way == 0 else -1)
        return remote(ref, ref, send.at[part, stage, way, k], recv.at[part, stage, way, k], device)

    def across(part, stage, way, k, side):
        ref = arrived(part, stage, way, k, side)
        at = (part, stage, way, k)
        return remote(ref, ref, pair_send.at[at], pair_recv.at[at], place.partner())

    cast_ref[...] = own_ref[...].astype(cast_ref.dtype)
    place.greet()
    steps = [(part, way) for part in range(3) for way in range(2)]
    for k in range(2):
        for part, way in steps:
            outgoing(part, 0, way, k).start()
    mine = pltpu.make_async_copy(cast_ref, table_ref.at[x, y, core, z], local_sem)
    mine.start()
    own = remote(cast_ref, table_ref.at[x, y, core, z], own_sem.at[0], own_sem.at[1], place.partner())
    own.start()
    mine.wait()
    for stage in range(3):
        for k in range(3):
            for part in range(3):
                for way in range(2):
                    incoming(part, stage, way, k).wait_recv()
                    if k == 0:
                        outgoing(part, stage, way, 2).start()
                    across(part, stage, way, k, core).start()
                if k == 2 and stage < 2:
                    for way in range(2):
                        outgoing(part, stage + 1, way, 0).start()
                        outgoing(part, stage + 1, way, 1).start()
    own.wait_send()
    theirs = table_ref.at[x, y, other, z]
    remote(theirs, theirs, own_sem.at[0], own_sem.at[1], place.partner()).wait_recv()
    for stage in range(3):
        for k in range(3):
            for part, way in steps:
                outgoing(part, stage, way, k).wait_send()
                across(part, stage, way, k, core).wait_send()
                across(part, stage, way, k, other).wait_recv()


def gather_rows(factors):
    modes, rows, rank = factors.shape
    return pl.pallas_call(
        gather_kernel,
        out_shape=jax.ShapeDtypeStruct((4, 4, 2, 4, modes, rows, rank), jnp.bfloat16),
        in_specs=[pl.BlockSpec(memory_space=pltpu.VMEM)],
        out_specs=pl.BlockSpec(memory_space=pl.ANY),
        scratch_shapes=[
            pltpu.VMEM((modes, rows, rank), jnp.bfloat16),
            pltpu.SemaphoreType.DMA,
            pltpu.SemaphoreType.DMA((2,)),
            pltpu.SemaphoreType.DMA((3, 3, 2, 3)),
            pltpu.SemaphoreType.DMA((3, 3, 2, 3)),
            pltpu.SemaphoreType.DMA((3, 3, 2, 3)),
            pltpu.SemaphoreType.DMA((3, 3, 2, 3)),
        ],
        compiler_params=pltpu.CompilerParams(collective_id=0, has_side_effects=True),
    )(factors)


GROUP = 4
CHUNK = 16


def block_part(rows_ref, block_ref):
    _, edge, rank = rows_ref.shape
    half_a = rows_ref[0] * jnp.bfloat16(0.5)
    rows_c = rows_ref[2]
    width = CHUNK * edge
    twice = lambda rows: jnp.concatenate([rows, rows], axis=0).astype(jnp.float32).T
    cols_b = twice(rows_ref[1])
    cols_c = twice(rows_c).astype(jnp.bfloat16)
    lane = lax.broadcasted_iota(jnp.int32, (rank, 2 * edge), 1)
    total = jnp.zeros((edge, rank), jnp.float32)
    for step in range(edge // CHUNK):
        pair = jnp.concatenate(
            [rows_ref[1, pl.ds(step * CHUNK + j, 1), :] * rows_c for j in range(CHUNK)], axis=0
        )
        if step == 0:
            model = lax.dot_general(
                half_a, pair, (((1,), (1,)), ((), ())), preferred_element_type=jnp.float32
            )
        else:
            pieces = []
            for j in range(step * CHUNK, (step + 1) * CHUNK, 2):
                pick = jnp.where(lane < edge, j, j + 1)
                spread = jnp.take_along_axis(cols_b, pick, axis=1).astype(jnp.bfloat16)
                pieces.append(spread * cols_c)
            model = jnp.dot(
                half_a, jnp.concatenate(pieces, axis=1), preferred_element_type=jnp.float32
            )
        observed = block_ref[:, step * width : (step + 1) * width].astype(jnp.float32)
        resid = (0.5 * jnp.tanh(model) + (0.5 - observed)).astype(jnp.bfloat16)
        total = total + jnp.dot(resid, pair, preferred_element_type=jnp.float32)
    return total


def block_kernel(
    local_blocks, coords_ref, owner_ref, count_ref, blocks_ref, table_ref, parts_ref, slot_ref,
    block_buf, rows_buf, part_buf, row_of, block_sems, rows_sems, part_sems,
):
    slots = blocks_ref.shape[0]
    modes = rows_buf.shape[2]
    count = count_ref[0]
    groups = lax.div(count + (GROUP - 1), GROUP)

    def block_copy(h):
        at = lax.rem(h, 2)
        return pltpu.make_async_copy(
            blocks_ref.at[pl.ds(h * GROUP, GROUP)], block_buf.at[at], block_sems.at[at]
        )

    def start_rows(h):
        at = lax.rem(h, 2)
        for q in range(GROUP):
            for m in range(modes):
                pltpu.make_async_copy(
                    table_ref.at[row_of[m, h * GROUP + q]], rows_buf.at[at, q, m], rows_sems.at[at]
                ).start()

    def wait_rows(h):
        at = lax.rem(h, 2)
        pltpu.make_async_copy(rows_buf.at[at], rows_buf.at[at], rows_sems.at[at]).wait()

    def store(h):
        span = pl.ds(h * GROUP, GROUP)
        return pltpu.make_async_copy(part_buf.at[span], parts_ref.at[span], part_sems.at[h])

    last = pltpu.make_async_copy(
        part_buf.at[slots], parts_ref.at[slots], part_sems.at[slots // GROUP]
    )

    block_copy(0).start()

    @pl.loop(0, slots)
    def _(s):
        for m in range(modes):
            pos = owner_ref[m, coords_ref[m, s]]
            row_of[m, s] = (
                lax.div(pos, local_blocks) * modes + m
            ) * local_blocks + lax.rem(pos, local_blocks)

    start_rows(0)

    @pl.loop(0, slot_ref.shape[0])
    def _(p):
        slot_ref[p] = slots

    @pl.loop(0, count)
    def _(s):
        slot_ref[owner_ref[0, coords_ref[0, s]]] = s

    part_buf[slots] = jnp.zeros(part_buf.shape[1:], jnp.float32)
    last.start()

    @pl.loop(0, groups)
    def _(h):
        at = lax.rem(h, 2)

        @pl.when(h + 1 < groups)
        def _():
            block_copy(h + 1).start()
            start_rows(h + 1)

        block_copy(h).wait()
        wait_rows(h)
        for q in range(GROUP):
            part_buf[h * GROUP + q] = block_part(rows_buf.at[at, q], block_buf.at[at, q])
        store(h).start()

    @pl.loop(0, groups)
    def _(h):
        store(h).wait()

    last.wait()


def block_gradients(tensor_blocks, table, coords, owner, count, positions, local_blocks):
    slots, edge, merged = tensor_blocks.shape
    modes, _ = coords.shape
    rank = table.shape[2]
    smem = pl.BlockSpec(memory_space=pltpu.SMEM)
    far = pl.BlockSpec(memory_space=pltpu.HBM)
    return pl.pallas_call(
        functools.partial(block_kernel, local_blocks),
        out_shape=(
            jax.ShapeDtypeStruct((slots + 1, edge, rank), jnp.float32),
            jax.ShapeDtypeStruct((positions,), jnp.int32),
        ),
        in_specs=[smem, smem, smem, far, far],
        out_specs=(far, smem),
        scratch_shapes=[
            pltpu.VMEM((2, GROUP, edge, merged), jnp.bfloat16),
            pltpu.VMEM((2, GROUP, modes, edge, rank), jnp.bfloat16),
            pltpu.VMEM((slots + 1, edge, rank), jnp.float32),
            pltpu.SMEM((modes, slots), jnp.int32),
            pltpu.SemaphoreType.DMA((2,)),
            pltpu.SemaphoreType.DMA((2,)),
            pltpu.SemaphoreType.DMA((slots // GROUP + 1,)),
        ],
        compiler_params=pltpu.CompilerParams(vmem_limit_bytes=62 << 20),
        cost_estimate=pl.CostEstimate(
            flops=4 * slots * edge * merged * rank,
            bytes_accessed=2 * slots * edge * (merged + 5 * rank),
            transcendentals=slots * edge * merged,
        ),
    )(coords, owner, count, tensor_blocks, table)


CUTS = (((0, 88), (0, 128)), ((0, 88), (128, 256)), ((88, 128), (0, 256)))
SPLITS = ((48, 40), (48, 40), (24, 16))


def half_shape(part, stage):
    (r0, r1), (c0, c1) = CUTS[part]
    if stage == 2:
        return (SPLITS[part][0], c1 - c0)
    return ((8 if stage == 0 else 2) * (r1 - r0) + 16, c1 - c0)


def half_type(stage):
    return jnp.float32 if stage == 2 else jnp.int16


LEVELS = 32767.0


def scatter_kernel(slot_ref, parts_ref, grad_ref, acc, outbox, inbox, *rest):
    landed = rest[:9]
    packed = rest[9:15]
    send, recv, pair_send, pair_recv = rest[15:]
    place = Place()
    edge = parts_ref.shape[1]

    def spans(part, stage, k, half):
        order = ORDERS[part]
        (r0, r1), (c0, c1) = CUTS[part]
        index = [slice(0, RING)] * 3
        for axis in order[:stage]:
            index[axis] = 0
        index[order[stage]] = k
        if half is not None:
            if stage < 2:
                index[order[stage + 1]] = slice(2 * half, 2 * half + 2)
            else:
                cut = r0 + SPLITS[part][0]
                r0, r1 = (r0, cut) if half == 0 else (cut, r1)
        return index, slice(r0, r1), slice(c0, c1)

    def region(ref, part, stage, k, half):
        index, rows, cols = spans(part, stage, k, half)
        return ref.at[index[0], index[1], index[2], rows, cols]

    def cells(part, stage, k, half):
        index, rows, cols = spans(part, stage, k, half)
        each = [range(i.start, i.stop) if isinstance(i, slice) else (i,) for i in index]
        return [acc.at[x, y, z, rows, cols] for x in each[0] for y in each[1] for z in each[2]]

    def half_of(way, k):
        return way if k != 1 else 1 - way

    def landing(part, stage, way, k):
        ref = landed[part * 3 + stage].at[way, k]
        if stage == 2:
            ref = ref.at[0 : SPLITS[part][half_of(way, k)]]
        return ref

    def source(part, stage, way, k):
        if stage < 2:
            return packed[part * 2 + stage].at[way, k]
        return region(acc, part, stage, 2 if k == 0 else (3 if way == 0 else 1), half_of(way, k))

    def transfer(part, stage, way, k):
        device = place.neighbour(ORDERS[part][stage], -1 if way == 0 else 1)
        at = (part, stage, way, k)
        return remote(
            source(part, stage, way, k), landing(part, stage, way, k), send.at[at], recv.at[at], device
        )

    def emit(part, stage, way, k):
        if stage < 2:
            refs = cells(part, stage, 2 if k == 0 else (3 if way == 0 else 1), half_of(way, k))
            rows = refs[0].shape[0]
            peak = jnp.abs(refs[0][...])
            for ref in refs[1:]:
                peak = jnp.maximum(peak, jnp.abs(ref[...]))
            peak = jnp.maximum(jnp.max(peak, axis=0, keepdims=True), 1e-30)
            power = jnp.ceil(jnp.log2(peak))
            factor = jnp.exp2(-power) * LEVELS
            out = source(part, stage, way, k)
            for i in range(0, len(refs), 2):
                both = jnp.concatenate([refs[i][...], refs[i + 1][...]], axis=0)
                out[i * rows : (i + 2) * rows, :] = (
                    jnp.round(both * factor).astype(jnp.int32).astype(jnp.int16)
                )
            out[len(refs) * rows :, :] = jnp.broadcast_to(
                power, (16, power.shape[1])
            ).astype(jnp.int32).astype(jnp.int16)
        transfer(part, stage, way, k).start()

    def take(part, stage, way, k):
        transfer(part, stage, way, k).wait_recv()
        refs = cells(part, stage, (3 if way == 0 else 1) if k == 0 else 0, half_of(way, k))
        came = landing(part, stage, way, k)
        if stage == 2:
            refs[0][...] = refs[0][...] + came[...]
            return
        rows = refs[0].shape[0]
        power = came[len(refs) * rows :, :].astype(jnp.int32).astype(jnp.float32)[:1]
        factor = jnp.exp2(power) * (1.0 / LEVELS)
        for i in range(0, len(refs), 2):
            both = came[i * rows : (i + 2) * rows, :].astype(jnp.int32).astype(jnp.float32) * factor
            refs[i][...] = refs[i][...] + both[:rows]
            refs[i + 1][...] = refs[i + 1][...] + both[rows:]

    def across(part, k):
        at = (part, k)
        return remote(
            region(outbox, part, 0, k, None),
            region(inbox, part, 0, k, None),
            pair_send.at[at],
            pair_recv.at[at],
            place.partner(),
        )

    def take_across(part, k):
        across(part, k).wait_recv()
        target = region(acc, part, 0, k, None)
        target[...] = target[...] + region(inbox, part, 0, k, None)[...]

    def spread(ref, core):
        @pl.loop(0, RING**3)
        def _(r):
            step = (lax.div(r, 16), lax.rem(lax.div(r, 4), 4), lax.rem(r, 4))
            blk, grp = place.device(
                [lax.rem(v + s, RING) for v, s in zip(place.coord, step)], core
            )
            first = (blk * 4 + grp) * 2
            for j in range(2):
                ref[step[0], step[1], step[2], j * edge : (j + 1) * edge, :] = parts_ref[
                    slot_ref[first + j]
                ]

    place.announce()
    spread(outbox, 1 - place.core)
    place.await_peers()
    for k in (2, 3, 1, 0):
        for part in range(3):
            across(part, k).start()
    spread(acc, place.core)
    for part in range(3):
        take_across(part, 2)
        for way in range(2):
            emit(part, 0, way, 0)
    for part in range(3):
        for way, k in ((0, 3), (1, 1)):
            take_across(part, k)
            emit(part, 0, way, 1)
    for stage in range(3):
        for part in range(3):
            for way in range(2):
                take(part, stage, way, 0)
                emit(part, stage, way, 2)
        if stage == 0:
            for part in range(3):
                take_across(part, 0)
        for part in range(3):
            for k in (1, 2):
                for way in range(2):
                    take(part, stage, way, k)
            if stage < 2:
                for k in range(2):
                    for way in range(2):
                        emit(part, stage + 1, way, k)
    grad_ref[...] = acc[0, 0, 0]
    for part in range(3):
        for k in range(4):
            across(part, k).wait_send()
        for stage in range(3):
            for way in range(2):
                for k in range(3):
                    transfer(part, stage, way, k).wait_send()


def scatter_gradients(parts, slot_of):
    edge, rank = parts.shape[1:]
    dense = (RING, RING, RING, 2 * edge, rank)
    buffers = [
        pltpu.VMEM((2, 3) + half_shape(part, stage), half_type(stage))
        for stages in (range(3), range(2))
        for part in range(3)
        for stage in stages
    ]
    return pl.pallas_call(
        scatter_kernel,
        out_shape=jax.ShapeDtypeStruct((2 * edge, rank), jnp.float32),
        in_specs=[
            pl.BlockSpec(memory_space=pltpu.SMEM),
            pl.BlockSpec(memory_space=pltpu.VMEM),
        ],
        out_specs=pl.BlockSpec(memory_space=pltpu.VMEM),
        scratch_shapes=[pltpu.VMEM(dense, jnp.float32)] * 3
        + buffers
        + [
            pltpu.SemaphoreType.DMA((3, 3, 2, 3)),
            pltpu.SemaphoreType.DMA((3, 3, 2, 3)),
            pltpu.SemaphoreType.DMA((3, 4)),
            pltpu.SemaphoreType.DMA((3, 4)),
        ],
        compiler_params=pltpu.CompilerParams(
            collective_id=1, has_side_effects=True, vmem_limit_bytes=62 << 20
        ),
    )(slot_of, parts)


def per_device(tensor_blocks, block_coords, block_count, row_owner, factors, moment1, moment2):
    edge = tensor_blocks.shape[1]
    modes, local_rows, rank = factors.shape
    local_blocks = local_rows // edge
    positions = lax.axis_size(AXES) * local_blocks
    table = gather_rows(factors).reshape(modes * positions, edge, rank)
    parts, slot_of = block_gradients(
        tensor_blocks, table, block_coords, row_owner, block_count, positions, local_blocks
    )
    grad = scatter_gradients(parts, slot_of)
    new_moment1 = 0.9 * moment1 + 0.1 * grad
    new_moment2 = 0.999 * moment2 + 0.001 * grad * grad
    new_factor = factors[0] - 0.02 * (new_moment1 / (1.0 - 0.9**8)) / (
        jnp.sqrt(new_moment2 / (1.0 - 0.999**8)) + 1e-08
    )
    return (new_factor, new_moment1, new_moment2)


def solution(mesh):
    return jax.shard_map(
        per_device,
        mesh=mesh,
        in_specs=(
            P(AXES, None, None),
            P(None, AXES),
            P(AXES),
            P(),
            P(None, AXES, None),
            P(AXES, None),
            P(AXES, None),
        ),
        out_specs=(P(AXES, None), P(AXES, None), P(AXES, None)),
        check_vma=False,
    )
```

```python
import functools

import jax
import jax.numpy as jnp
from jax import lax
from jax.experimental import pallas as pl
from jax.experimental.pallas import tpu as pltpu
from jax.sharding import PartitionSpec as P

AXES = ("blk", "grp")
MESH = pl.DeviceIdType.MESH
RING = 4
ORDERS = ((0, 1, 2), (1, 2, 0), (2, 0, 1))


class Place:
    def __init__(self):
        blk = lax.axis_index("blk")
        self.coord = [lax.div(blk, 8), lax.rem(lax.div(blk, 2), 4), lax.axis_index("grp")]
        self.core = lax.rem(blk, 2)

    @staticmethod
    def device(coord, core):
        return (coord[0] * 8 + coord[1] * 2 + core, coord[2])

    def partner(self):
        return self.device(self.coord, 1 - self.core)

    def along(self, axis, step):
        return lax.rem(self.coord[axis] + (RING + step), RING)

    def neighbour(self, axis, step):
        coord = list(self.coord)
        coord[axis] = self.along(axis, step)
        return self.device(coord, self.core)

    def greet(self):
        self.announce()
        self.await_peers()

    def announce(self):
        barrier = pltpu.get_barrier_semaphore()
        peers = [self.neighbour(axis, step) for axis in range(3) for step in (1, -1)]
        for peer in peers + [self.partner()]:
            pl.semaphore_signal(barrier, inc=1, device_id=peer, device_id_type=MESH)

    def await_peers(self):
        pl.semaphore_wait(pltpu.get_barrier_semaphore(), 7)


def remote(src, dst, send, recv, device):
    return pltpu.make_async_remote_copy(
        src_ref=src, dst_ref=dst, send_sem=send, recv_sem=recv, device_id=device, device_id_type=MESH
    )


def gather_kernel(own_ref, table_ref, cast_ref, local_sem, own_sem, send, recv, pair_send, pair_recv):
    place = Place()
    x, y, z = place.coord
    core = place.core
    other = 1 - core
    half_rows = cast_ref.shape[1] // 2

    def region(part, stage, value, half, side, piece=None):
        order = ORDERS[part]
        index = list(place.coord)
        for axis in order[:stage]:
            index[axis] = slice(None)
        if piece is not None:
            index[order[stage - 1]] = piece
        index[order[stage]] = value
        return table_ref.at[
            index[0], index[1], side, index[2], part, half * half_rows : (half + 1) * half_rows
        ]

    def passed(stage):
        return range(2, 3) if stage < 2 else range(2, 2 + RING)

    def piece_of(stage, k):
        return k - 2 if stage == 2 and k >= 2 else None

    def arrived(part, stage, way, k, side):
        axis = ORDERS[part][stage]
        step = -1 if way == 0 else 1
        value = place.along(axis, step if k < 2 else 2)
        half = way if k != 1 else 1 - way
        return region(part, stage, value, half, side, piece_of(stage, k))

    def outgoing(part, stage, way, k):
        axis = ORDERS[part][stage]
        half = way if k != 1 else 1 - way
        if k < 2:
            dst = region(part, stage, place.coord[axis], half, core)
            src = dst
            if stage == 0:
                src = cast_ref.at[part, half * half_rows : (half + 1) * half_rows]
        else:
            value = place.along(axis, -1 if way == 0 else 1)
            dst = src = region(part, stage, value, half, core, piece_of(stage, k))
        device = place.neighbour(axis, 1 if way == 0 else -1)
        return remote(src, dst, send.at[part, stage, way, k], recv.at[part, stage, way, k], device)

    def incoming(part, stage, way, k):
        ref = arrived(part, stage, way, k, core)
        axis = ORDERS[part][stage]
        device = place.neighbour(axis, 1 if way == 0 else -1)
        return remote(ref, ref, send.at[part, stage, way, k], recv.at[part, stage, way, k], device)

    def across(part, stage, way, k, side):
        ref = arrived(part, stage, way, k, side)
        at = (part, stage, way, k)
        return remote(ref, ref, pair_send.at[at], pair_recv.at[at], place.partner())

    def drain(stage, ks):
        for k in ks:
            for part, way in steps:
                outgoing(part, stage, way, k).wait_send()
                across(part, stage, way, k, core).wait_send()
                across(part, stage, way, k, other).wait_recv()

    place.announce()
    cast_ref[...] = own_ref[...].astype(cast_ref.dtype)
    place.await_peers()
    steps = [(part, way) for part in range(3) for way in range(2)]
    for k in range(2):
        for part, way in steps:
            outgoing(part, 0, way, k).start()
    mine = pltpu.make_async_copy(cast_ref, table_ref.at[x, y, core, z], local_sem)
    mine.start()
    own = remote(cast_ref, table_ref.at[x, y, core, z], own_sem.at[0], own_sem.at[1], place.partner())
    own.start()
    mine.wait()
    for stage in range(3):
        for k in (0, 1) + tuple(passed(stage)):
            if stage == 2 and k == 1:
                own.wait_send()
                theirs = table_ref.at[x, y, other, z]
                remote(theirs, theirs, own_sem.at[0], own_sem.at[1], place.partner()).wait_recv()
                for before in range(2):
                    drain(before, (0, 1) + tuple(passed(before)))
            if stage == 2 and k == 2:
                drain(2, (0,))
            for part in range(3):
                for way in range(2):
                    incoming(part, stage, way, k).wait_recv()
                    if k == 0:
                        for later in passed(stage):
                            outgoing(part, stage, way, later).start()
                    across(part, stage, way, k, core).start()
                if k == 2 and stage < 2:
                    for way in range(2):
                        outgoing(part, stage + 1, way, 0).start()
                        outgoing(part, stage + 1, way, 1).start()
    drain(2, (1,) + tuple(passed(2)))


def gather_rows(factors):
    modes, rows, rank = factors.shape
    return pl.pallas_call(
        gather_kernel,
        out_shape=jax.ShapeDtypeStruct((4, 4, 2, 4, modes, rows, rank), jnp.bfloat16),
        in_specs=[pl.BlockSpec(memory_space=pltpu.VMEM)],
        out_specs=pl.BlockSpec(memory_space=pl.ANY),
        scratch_shapes=[
            pltpu.VMEM((modes, rows, rank), jnp.bfloat16),
            pltpu.SemaphoreType.DMA,
            pltpu.SemaphoreType.DMA((2,)),
            pltpu.SemaphoreType.DMA((3, 3, 2, 2 + RING)),
            pltpu.SemaphoreType.DMA((3, 3, 2, 2 + RING)),
            pltpu.SemaphoreType.DMA((3, 3, 2, 2 + RING)),
            pltpu.SemaphoreType.DMA((3, 3, 2, 2 + RING)),
        ],
        compiler_params=pltpu.CompilerParams(collective_id=0, has_side_effects=True),
    )(factors)


GROUP = 4
CHUNK = 16


def block_part(rows_ref, block_ref):
    _, edge, rank = rows_ref.shape
    half_a = rows_ref[0] * jnp.bfloat16(0.5)
    rows_c = rows_ref[2]
    width = CHUNK * edge
    twice = lambda rows: jnp.concatenate([rows, rows], axis=0).astype(jnp.float32).T
    cols_b = twice(rows_ref[1])
    cols_c = twice(rows_c).astype(jnp.bfloat16)
    lane = lax.broadcasted_iota(jnp.int32, (rank, 2 * edge), 1)
    total = jnp.zeros((edge, rank), jnp.float32)
    for step in range(edge // CHUNK):
        pair = jnp.concatenate(
            [rows_ref[1, pl.ds(step * CHUNK + j, 1), :] * rows_c for j in range(CHUNK)], axis=0
        )
        if step == 0:
            model = lax.dot_general(
                half_a, pair, (((1,), (1,)), ((), ())), preferred_element_type=jnp.float32
            )
        else:
            pieces = []
            for j in range(step * CHUNK, (step + 1) * CHUNK, 2):
                pick = jnp.where(lane < edge, j, j + 1)
                spread = jnp.take_along_axis(cols_b, pick, axis=1).astype(jnp.bfloat16)
                pieces.append(spread * cols_c)
            model = jnp.dot(
                half_a, jnp.concatenate(pieces, axis=1), preferred_element_type=jnp.float32
            )
        observed = block_ref[:, step * width : (step + 1) * width].astype(jnp.float32)
        resid = (0.5 * jnp.tanh(model) + (0.5 - observed)).astype(jnp.bfloat16)
        total = total + jnp.dot(resid, pair, preferred_element_type=jnp.float32)
    return total


def block_kernel(
    local_blocks, coords_ref, owner_ref, count_ref, blocks_ref, table_ref, parts_ref, slot_ref,
    block_buf, rows_buf, part_buf, row_of, block_sems, rows_sems, part_sems,
):
    slots = blocks_ref.shape[0]
    modes = rows_buf.shape[2]
    count = count_ref[0]
    groups = lax.div(count + (GROUP - 1), GROUP)

    def block_copy(h):
        at = lax.rem(h, 2)
        return pltpu.make_async_copy(
            blocks_ref.at[pl.ds(h * GROUP, GROUP)], block_buf.at[at], block_sems.at[at]
        )

    def start_rows(h):
        at = lax.rem(h, 2)
        for q in range(GROUP):
            for m in range(modes):
                pltpu.make_async_copy(
                    table_ref.at[row_of[m, h * GROUP + q]], rows_buf.at[at, q, m], rows_sems.at[at]
                ).start()

    def wait_rows(h):
        at = lax.rem(h, 2)
        pltpu.make_async_copy(rows_buf.at[at], rows_buf.at[at], rows_sems.at[at]).wait()

    def store(h):
        span = pl.ds(h * GROUP, GROUP)
        return pltpu.make_async_copy(part_buf.at[span], parts_ref.at[span], part_sems.at[h])

    last = pltpu.make_async_copy(
        part_buf.at[slots], parts_ref.at[slots], part_sems.at[slots // GROUP]
    )

    block_copy(0).start()

    def look_up(s):
        for m in range(modes):
            pos = owner_ref[m, coords_ref[m, s]]
            row_of[m, s] = (
                lax.div(pos, local_blocks) * modes + m
            ) * local_blocks + lax.rem(pos, local_blocks)

    for s in range(GROUP):
        look_up(s)
    start_rows(0)

    @pl.loop(GROUP, slots)
    def _(s):
        look_up(s)

    @pl.loop(0, slot_ref.shape[0])
    def _(p):
        slot_ref[p] = slots

    @pl.loop(0, count)
    def _(s):
        slot_ref[owner_ref[0, coords_ref[0, s]]] = s

    part_buf[slots] = jnp.zeros(part_buf.shape[1:], jnp.float32)
    last.start()

    @pl.loop(0, groups)
    def _(h):
        at = lax.rem(h, 2)

        @pl.when(h + 1 < groups)
        def _():
            block_copy(h + 1).start()
            start_rows(h + 1)

        block_copy(h).wait()
        wait_rows(h)
        for q in range(GROUP):
            part_buf[h * GROUP + q] = block_part(rows_buf.at[at, q], block_buf.at[at, q])
        store(h).start()

    @pl.loop(0, groups)
    def _(h):
        store(h).wait()

    last.wait()


def block_gradients(tensor_blocks, table, coords, owner, count, positions, local_blocks):
    slots, edge, merged = tensor_blocks.shape
    modes, _ = coords.shape
    rank = table.shape[2]
    smem = pl.BlockSpec(memory_space=pltpu.SMEM)
    far = pl.BlockSpec(memory_space=pltpu.HBM)
    return pl.pallas_call(
        functools.partial(block_kernel, local_blocks),
        out_shape=(
            jax.ShapeDtypeStruct((slots + 1, edge, rank), jnp.float32),
            jax.ShapeDtypeStruct((positions,), jnp.int32),
        ),
        in_specs=[smem, smem, smem, far, far],
        out_specs=(far, smem),
        scratch_shapes=[
            pltpu.VMEM((2, GROUP, edge, merged), jnp.bfloat16),
            pltpu.VMEM((2, GROUP, modes, edge, rank), jnp.bfloat16),
            pltpu.VMEM((slots + 1, edge, rank), jnp.float32),
            pltpu.SMEM((modes, slots), jnp.int32),
            pltpu.SemaphoreType.DMA((2,)),
            pltpu.SemaphoreType.DMA((2,)),
            pltpu.SemaphoreType.DMA((slots // GROUP + 1,)),
        ],
        compiler_params=pltpu.CompilerParams(vmem_limit_bytes=62 << 20),
        cost_estimate=pl.CostEstimate(
            flops=4 * slots * edge * merged * rank,
            bytes_accessed=2 * slots * edge * (merged + 5 * rank),
            transcendentals=slots * edge * merged,
        ),
    )(coords, owner, count, tensor_blocks, table)


CUTS = (((0, 88), (0, 128)), ((0, 88), (128, 256)), ((88, 128), (0, 256)))
SPLITS = ((48, 40), (48, 40), (24, 16))


def half_shape(part, stage):
    (r0, r1), (c0, c1) = CUTS[part]
    if stage == 2:
        return (SPLITS[part][0], c1 - c0)
    return ((8 if stage == 0 else 2) * (r1 - r0) + 16, c1 - c0)


def half_type(stage):
    return jnp.float32 if stage == 2 else jnp.int16


LEVELS = 32767.0


def scatter_kernel(slot_ref, parts_ref, grad_ref, acc, outbox, inbox, *rest):
    landed = rest[:9]
    packed = rest[9:15]
    send, recv, pair_send, pair_recv = rest[15:]
    place = Place()
    edge = parts_ref.shape[1]

    def spans(part, stage, k, half):
        order = ORDERS[part]
        (r0, r1), (c0, c1) = CUTS[part]
        index = [slice(0, RING)] * 3
        for axis in order[:stage]:
            index[axis] = 0
        index[order[stage]] = k
        if half is not None:
            if stage < 2:
                index[order[stage + 1]] = slice(2 * half, 2 * half + 2)
            else:
                cut = r0 + SPLITS[part][0]
                r0, r1 = (r0, cut) if half == 0 else (cut, r1)
        return index, slice(r0, r1), slice(c0, c1)

    def region(ref, part, stage, k, half):
        index, rows, cols = spans(part, stage, k, half)
        return ref.at[index[0], index[1], index[2], rows, cols]

    def cells(part, stage, k, half):
        index, rows, cols = spans(part, stage, k, half)
        each = [range(i.start, i.stop) if isinstance(i, slice) else (i,) for i in index]
        return [acc.at[x, y, z, rows, cols] for x in each[0] for y in each[1] for z in each[2]]

    def half_of(way, k):
        return way if k != 1 else 1 - way

    def landing(part, stage, way, k):
        ref = landed[part * 3 + stage].at[way, k]
        if stage == 2:
            ref = ref.at[0 : SPLITS[part][half_of(way, k)]]
        return ref

    def source(part, stage, way, k):
        if stage < 2:
            return packed[part * 2 + stage].at[way, k]
        return region(acc, part, stage, 2 if k == 0 else (3 if way == 0 else 1), half_of(way, k))

    def transfer(part, stage, way, k):
        device = place.neighbour(ORDERS[part][stage], -1 if way == 0 else 1)
        at = (part, stage, way, k)
        return remote(
            source(part, stage, way, k), landing(part, stage, way, k), send.at[at], recv.at[at], device
        )

    def emit(part, stage, way, k):
        if stage < 2:
            refs = cells(part, stage, 2 if k == 0 else (3 if way == 0 else 1), half_of(way, k))
            rows = refs[0].shape[0]
            peak = jnp.abs(refs[0][...])
            for ref in refs[1:]:
                peak = jnp.maximum(peak, jnp.abs(ref[...]))
            peak = jnp.maximum(jnp.max(peak, axis=0, keepdims=True), 1e-30)
            power = jnp.ceil(jnp.log2(peak))
            factor = jnp.exp2(-power) * LEVELS
            out = source(part, stage, way, k)
            for i in range(0, len(refs), 2):
                both = jnp.concatenate([refs[i][...], refs[i + 1][...]], axis=0)
                out[i * rows : (i + 2) * rows, :] = (
                    jnp.round(both * factor).astype(jnp.int32).astype(jnp.int16)
                )
            out[len(refs) * rows :, :] = jnp.broadcast_to(
                power, (16, power.shape[1])
            ).astype(jnp.int32).astype(jnp.int16)
        transfer(part, stage, way, k).start()

    def take(part, stage, way, k):
        transfer(part, stage, way, k).wait_recv()
        refs = cells(part, stage, (3 if way == 0 else 1) if k == 0 else 0, half_of(way, k))
        came = landing(part, stage, way, k)
        if stage == 2:
            refs[0][...] = refs[0][...] + came[...]
            return
        rows = refs[0].shape[0]
        power = came[len(refs) * rows :, :].astype(jnp.int32).astype(jnp.float32)[:1]
        factor = jnp.exp2(power) * (1.0 / LEVELS)
        for i in range(0, len(refs), 2):
            both = came[i * rows : (i + 2) * rows, :].astype(jnp.int32).astype(jnp.float32) * factor
            refs[i][...] = refs[i][...] + both[:rows]
            refs[i + 1][...] = refs[i + 1][...] + both[rows:]

    def across(part, k):
        at = (part, k)
        return remote(
            region(outbox, part, 0, k, None),
            region(inbox, part, 0, k, None),
            pair_send.at[at],
            pair_recv.at[at],
            place.partner(),
        )

    def take_across(part, k):
        across(part, k).wait_recv()
        target = region(acc, part, 0, k, None)
        target[...] = target[...] + region(inbox, part, 0, k, None)[...]

    def spread(ref, core):
        @pl.loop(0, RING**3)
        def _(r):
            step = (lax.div(r, 16), lax.rem(lax.div(r, 4), 4), lax.rem(r, 4))
            blk, grp = place.device(
                [lax.rem(v + s, RING) for v, s in zip(place.coord, step)], core
            )
            first = (blk * 4 + grp) * 2
            for j in range(2):
                ref[step[0], step[1], step[2], j * edge : (j + 1) * edge, :] = parts_ref[
                    slot_ref[first + j]
                ]

    def sent(part, stage):
        for way in range(2):
            for k in range(3):
                transfer(part, stage, way, k).wait_send()

    place.announce()
    spread(outbox, 1 - place.core)
    place.await_peers()
    for k in (2, 3, 1, 0):
        for part in range(3):
            across(part, k).start()
    spread(acc, place.core)
    for part in range(3):
        take_across(part, 2)
        for way in range(2):
            emit(part, 0, way, 0)
    for part in range(3):
        for way, k in ((0, 3), (1, 1)):
            take_across(part, k)
            emit(part, 0, way, 1)
    for stage in range(3):
        for part in range(3):
            for way in range(2):
                take(part, stage, way, 0)
                emit(part, stage, way, 2)
        if stage == 0:
            for part in range(3):
                take_across(part, 0)
        if stage == 2:
            for part in range(3):
                for k in range(4):
                    across(part, k).wait_send()
                for before in range(2):
                    sent(part, before)
        for part in range(3):
            for k in (1, 2):
                for way in range(2):
                    take(part, stage, way, k)
            if stage < 2:
                for k in range(2):
                    for way in range(2):
                        emit(part, stage + 1, way, k)
    grad_ref[...] = acc[0, 0, 0]
    for part in range(3):
        sent(part, 2)


def scatter_gradients(parts, slot_of):
    edge, rank = parts.shape[1:]
    dense = (RING, RING, RING, 2 * edge, rank)
    buffers = [
        pltpu.VMEM((2, 3) + half_shape(part, stage), half_type(stage))
        for stages in (range(3), range(2))
        for part in range(3)
        for stage in stages
    ]
    return pl.pallas_call(
        scatter_kernel,
        out_shape=jax.ShapeDtypeStruct((2 * edge, rank), jnp.float32),
        in_specs=[
            pl.BlockSpec(memory_space=pltpu.SMEM),
            pl.BlockSpec(memory_space=pltpu.VMEM),
        ],
        out_specs=pl.BlockSpec(memory_space=pltpu.VMEM),
        scratch_shapes=[pltpu.VMEM(dense, jnp.float32)] * 3
        + buffers
        + [
            pltpu.SemaphoreType.DMA((3, 3, 2, 3)),
            pltpu.SemaphoreType.DMA((3, 3, 2, 3)),
            pltpu.SemaphoreType.DMA((3, 4)),
            pltpu.SemaphoreType.DMA((3, 4)),
        ],
        compiler_params=pltpu.CompilerParams(
            collective_id=1, has_side_effects=True, vmem_limit_bytes=62 << 20
        ),
    )(slot_of, parts)


def per_device(tensor_blocks, block_coords, block_count, row_owner, factors, moment1, moment2):
    edge = tensor_blocks.shape[1]
    modes, local_rows, rank = factors.shape
    local_blocks = local_rows // edge
    positions = lax.axis_size(AXES) * local_blocks
    table = gather_rows(factors).reshape(modes * positions, edge, rank)
    parts, slot_of = block_gradients(
        tensor_blocks, table, block_coords, row_owner, block_count, positions, local_blocks
    )
    grad = scatter_gradients(parts, slot_of)
    new_moment1 = 0.9 * moment1 + 0.1 * grad
    new_moment2 = 0.999 * moment2 + 0.001 * grad * grad
    new_factor = factors[0] - 0.02 * (new_moment1 / (1.0 - 0.9**8)) / (
        jnp.sqrt(new_moment2 / (1.0 - 0.999**8)) + 1e-08
    )
    return (new_factor, new_moment1, new_moment2)


def solution(mesh):
    return jax.shard_map(
        per_device,
        mesh=mesh,
        in_specs=(
            P(AXES, None, None),
            P(None, AXES),
            P(AXES),
            P(),
            P(None, AXES, None),
            P(AXES, None),
            P(AXES, None),
        ),
        out_specs=(P(AXES, None), P(AXES, None), P(AXES, None)),
        check_vma=False,
    )
```

```python
import functools

import jax
import jax.numpy as jnp
from jax import lax
from jax.experimental import pallas as pl
from jax.experimental.pallas import tpu as pltpu
from jax.sharding import PartitionSpec as P

AXES = ("blk", "grp")
MESH = pl.DeviceIdType.MESH
RING = 4
ORDERS = ((0, 1, 2), (1, 2, 0), (2, 0, 1))


class Place:
    def __init__(self):
        blk = lax.axis_index("blk")
        self.coord = [lax.div(blk, 8), lax.rem(lax.div(blk, 2), 4), lax.axis_index("grp")]
        self.core = lax.rem(blk, 2)

    @staticmethod
    def device(coord, core):
        return (coord[0] * 8 + coord[1] * 2 + core, coord[2])

    def partner(self):
        return self.device(self.coord, 1 - self.core)

    def along(self, axis, step):
        return lax.rem(self.coord[axis] + (RING + step), RING)

    def neighbour(self, axis, step):
        coord = list(self.coord)
        coord[axis] = self.along(axis, step)
        return self.device(coord, self.core)

    def offset(self, device):
        blk = lax.div(device, RING)
        coord = (lax.div(blk, 8), lax.rem(lax.div(blk, 2), 4), lax.rem(device, RING))
        steps = [lax.rem(v - me + RING, RING) for v, me in zip(coord, self.coord)]
        side = lax.rem(lax.rem(blk, 2) + self.core, 2)
        return ((steps[0] * RING + steps[1]) * RING + steps[2]) * 2 + side

    def announce(self):
        barrier = pltpu.get_barrier_semaphore()
        peers = [self.neighbour(axis, step) for axis in range(3) for step in (1, -1)]
        for peer in peers + [self.partner()]:
            pl.semaphore_signal(barrier, inc=1, device_id=peer, device_id_type=MESH)

    def await_peers(self):
        pl.semaphore_wait(pltpu.get_barrier_semaphore(), 7)


def remote(src, dst, send, recv, device):
    return pltpu.make_async_remote_copy(
        src_ref=src, dst_ref=dst, send_sem=send, recv_sem=recv, device_id=device, device_id_type=MESH
    )


ALL = slice(0, RING)
FAR = slice(1, RING)
GROUPS = (
    ((),),
    ((0,), (FAR,)),
    ((0, 0), (FAR, 0), (ALL, 1), (ALL, 3), (ALL, 2)),
)
LISTED = [(stage, g) for stage in range(3) for g in range(len(GROUPS[stage]))]
NUMBER = {at: i for i, at in enumerate(LISTED)}


def gather_kernel(own_ref, table_ref, cast_ref, local_sem, own_sem, send, recv, pair_send, pair_recv):
    place = Place()
    half_rows = cast_ref.shape[1] // 2

    def region(part, stage, g, value, half, side):
        index = [0, 0, 0]
        for axis, piece in zip(ORDERS[part], GROUPS[stage][g]):
            index[axis] = piece
        index[ORDERS[part][stage]] = value
        rows = slice(0, 2 * half_rows) if half is None else slice(half * half_rows, (half + 1) * half_rows)
        return table_ref.at[index[0], index[1], index[2], side, part, rows]

    def half_of(way, k):
        return way if k != 1 else 1 - way

    def copy(part, stage, g, way, k):
        half = half_of(way, k)
        came = 3 if way == 0 else 1
        if k == 2:
            src = region(part, stage, g, came, half, 0)
            dst = region(part, stage, g, 2, half, 0)
        else:
            src = region(part, stage, g, 0, half, 0)
            dst = region(part, stage, g, came, half, 0)
            if g == 0:
                src = cast_ref.at[part, half * half_rows : (half + 1) * half_rows]
        device = place.neighbour(ORDERS[part][stage], 1 if way == 0 else -1)
        at = (part, NUMBER[stage, g], way, k)
        return remote(src, dst, send.at[at], recv.at[at], device)

    def across(part, stage, g, way, j):
        value, half = ((3 if way == 0 else 1), None) if j == 0 else (2, way)
        at = (part, NUMBER[stage, g], way, j)
        return remote(
            region(part, stage, g, value, half, 0),
            region(part, stage, g, value, half, 1),
            pair_send.at[at],
            pair_recv.at[at],
            place.partner(),
        )

    steps = [(part, way) for part in range(3) for way in range(2)]

    def begin(stage, g):
        for k in range(2):
            for part, way in steps:
                copy(part, stage, g, way, k).start()

    def arrive(stage, g, k):
        for part, way in steps:
            copy(part, stage, g, way, k).wait_recv()
            if k == 0:
                copy(part, stage, g, way, 2).start()
            else:
                across(part, stage, g, way, k - 1).start()

    def drain(stage, g):
        for part, way in steps:
            for k in range(3):
                copy(part, stage, g, way, k).wait_send()
            for j in range(2):
                across(part, stage, g, way, j).wait_send()

    def collect(stage, g):
        for part, way in steps:
            for j in range(2):
                across(part, stage, g, way, j).wait_recv()

    place.announce()
    cast_ref[...] = own_ref[...].astype(cast_ref.dtype)
    place.await_peers()
    for stage in range(3):
        begin(stage, 0)
    mine = pltpu.make_async_copy(cast_ref, table_ref.at[0, 0, 0, 0], local_sem)
    mine.start()
    own = remote(cast_ref, table_ref.at[0, 0, 0, 1], own_sem.at[0], own_sem.at[1], place.partner())
    own.start()
    mine.wait()
    arrive(0, 0, 0)
    arrive(0, 0, 1)
    arrive(1, 0, 0)
    arrive(0, 0, 2)
    begin(1, 1)
    begin(2, 1)
    arrive(2, 0, 0)
    for k in range(1, 3):
        arrive(1, 0, k)
        arrive(2, 0, k)
    arrive(1, 1, 0)
    arrive(1, 1, 1)
    begin(2, 2)
    begin(2, 3)
    arrive(2, 1, 0)
    arrive(1, 1, 2)
    begin(2, 4)
    arrive(2, 1, 1)
    arrive(2, 1, 2)
    own.wait()
    for at in ((0, 0), (1, 0), (2, 0), (1, 1)):
        drain(*at)
        collect(*at)
    for g in (2, 3, 4):
        arrive(2, g, 0)
        arrive(2, g, 1)
    drain(2, 1)
    collect(2, 1)
    for g in (2, 3, 4):
        arrive(2, g, 2)
    for g in (2, 3, 4):
        drain(2, g)
        collect(2, g)


def gather_rows(factors):
    modes, rows, rank = factors.shape
    count = len(LISTED)
    return pl.pallas_call(
        gather_kernel,
        out_shape=jax.ShapeDtypeStruct((RING, RING, RING, 2, modes, rows, rank), jnp.bfloat16),
        in_specs=[pl.BlockSpec(memory_space=pltpu.VMEM)],
        out_specs=pl.BlockSpec(memory_space=pl.ANY),
        scratch_shapes=[
            pltpu.VMEM((modes, rows, rank), jnp.bfloat16),
            pltpu.SemaphoreType.DMA,
            pltpu.SemaphoreType.DMA((2,)),
            pltpu.SemaphoreType.DMA((3, count, 2, 3)),
            pltpu.SemaphoreType.DMA((3, count, 2, 3)),
            pltpu.SemaphoreType.DMA((3, count, 2, 2)),
            pltpu.SemaphoreType.DMA((3, count, 2, 2)),
        ],
        compiler_params=pltpu.CompilerParams(collective_id=0, has_side_effects=True),
    )(factors)


GROUP = 6
CHUNK = 16


def block_part(rows_ref, block_ref):
    _, edge, rank = rows_ref.shape
    half_a = rows_ref[0] * jnp.bfloat16(0.5)
    rows_c = rows_ref[2]
    width = CHUNK * edge
    twice = lambda rows: jnp.concatenate([rows, rows], axis=0).astype(jnp.float32).T
    cols_b = twice(rows_ref[1])
    cols_c = twice(rows_c).astype(jnp.bfloat16)
    lane = lax.broadcasted_iota(jnp.int32, (rank, 2 * edge), 1)
    total = jnp.zeros((edge, rank), jnp.float32)
    for step in range(edge // CHUNK):
        pair = jnp.concatenate(
            [rows_ref[1, pl.ds(step * CHUNK + j, 1), :] * rows_c for j in range(CHUNK)], axis=0
        )
        if step == 0:
            model = lax.dot_general(
                half_a, pair, (((1,), (1,)), ((), ())), preferred_element_type=jnp.float32
            )
        else:
            pieces = []
            for j in range(step * CHUNK, (step + 1) * CHUNK, 2):
                pick = jnp.where(lane < edge, j, j + 1)
                spread = jnp.take_along_axis(cols_b, pick, axis=1).astype(jnp.bfloat16)
                pieces.append(spread * cols_c)
            model = jnp.dot(
                half_a, jnp.concatenate(pieces, axis=1), preferred_element_type=jnp.float32
            )
        observed = block_ref[:, step * width : (step + 1) * width].astype(jnp.float32)
        resid = (0.5 * jnp.tanh(model) + (0.5 - observed)).astype(jnp.bfloat16)
        total = total + jnp.dot(resid, pair, preferred_element_type=jnp.float32)
    return total


def block_kernel(
    local_blocks, coords_ref, owner_ref, count_ref, blocks_ref, table_ref, parts_ref, slot_ref,
    block_buf, rows_buf, part_buf, row_of, block_sems, rows_sems, part_sems,
):
    slots = blocks_ref.shape[0]
    modes = rows_buf.shape[2]
    count = count_ref[0]
    place = Place()
    groups = lax.div(count + (GROUP - 1), GROUP)

    def block_copy(h):
        at = lax.rem(h, 2)
        return pltpu.make_async_copy(
            blocks_ref.at[pl.ds(h * GROUP, GROUP)], block_buf.at[at], block_sems.at[at]
        )

    def start_rows(h):
        at = lax.rem(h, 2)
        for q in range(GROUP):
            for m in range(modes):
                pltpu.make_async_copy(
                    table_ref.at[row_of[m, h * GROUP + q]], rows_buf.at[at, q, m], rows_sems.at[at]
                ).start()

    def wait_rows(h):
        at = lax.rem(h, 2)
        pltpu.make_async_copy(rows_buf.at[at], rows_buf.at[at], rows_sems.at[at]).wait()

    def store(h):
        span = pl.ds(h * GROUP, GROUP)
        return pltpu.make_async_copy(part_buf.at[span], parts_ref.at[span], part_sems.at[h])

    last = pltpu.make_async_copy(
        part_buf.at[slots], parts_ref.at[slots], part_sems.at[slots // GROUP]
    )

    block_copy(0).start()

    def look_up(s):
        for m in range(modes):
            pos = owner_ref[m, coords_ref[m, s]]
            row = (place.offset(lax.div(pos, local_blocks)) * modes + m) * local_blocks
            row_of[m, s] = row + lax.rem(pos, local_blocks)

    for s in range(GROUP):
        look_up(s)
    start_rows(0)

    @pl.loop(GROUP, slots)
    def _(s):
        look_up(s)

    @pl.loop(0, slot_ref.shape[0])
    def _(p):
        slot_ref[p] = slots

    @pl.loop(0, count)
    def _(s):
        slot_ref[owner_ref[0, coords_ref[0, s]]] = s

    part_buf[slots] = jnp.zeros(part_buf.shape[1:], jnp.float32)
    last.start()

    @pl.loop(0, groups)
    def _(h):
        at = lax.rem(h, 2)

        @pl.when(h + 1 < groups)
        def _():
            block_copy(h + 1).start()
            start_rows(h + 1)

        block_copy(h).wait()
        wait_rows(h)
        for q in range(GROUP):
            part_buf[h * GROUP + q] = block_part(rows_buf.at[at, q], block_buf.at[at, q])
        store(h).start()

    @pl.loop(0, groups)
    def _(h):
        store(h).wait()

    last.wait()


def block_gradients(tensor_blocks, table, coords, owner, count, positions, local_blocks):
    slots, edge, merged = tensor_blocks.shape
    modes, _ = coords.shape
    rank = table.shape[2]
    smem = pl.BlockSpec(memory_space=pltpu.SMEM)
    far = pl.BlockSpec(memory_space=pltpu.HBM)
    return pl.pallas_call(
        functools.partial(block_kernel, local_blocks),
        out_shape=(
            jax.ShapeDtypeStruct((slots + 1, edge, rank), jnp.float32),
            jax.ShapeDtypeStruct((positions,), jnp.int32),
        ),
        in_specs=[smem, smem, smem, far, far],
        out_specs=(far, smem),
        scratch_shapes=[
            pltpu.VMEM((2, GROUP, edge, merged), jnp.bfloat16),
            pltpu.VMEM((2, GROUP, modes, edge, rank), jnp.bfloat16),
            pltpu.VMEM((slots + 1, edge, rank), jnp.float32),
            pltpu.SMEM((modes, slots), jnp.int32),
            pltpu.SemaphoreType.DMA((2,)),
            pltpu.SemaphoreType.DMA((2,)),
            pltpu.SemaphoreType.DMA((slots // GROUP + 1,)),
        ],
        compiler_params=pltpu.CompilerParams(vmem_limit_bytes=62 << 20),
        cost_estimate=pl.CostEstimate(
            flops=4 * slots * edge * merged * rank,
            bytes_accessed=2 * slots * edge * (merged + 5 * rank),
            transcendentals=slots * edge * merged,
        ),
    )(coords, owner, count, tensor_blocks, table)


CUTS = (((0, 88), (0, 128)), ((0, 88), (128, 256)), ((88, 128), (0, 256)))
SPLITS = ((48, 40), (48, 40), (24, 16))


def half_shape(part, stage):
    (r0, r1), (c0, c1) = CUTS[part]
    if stage == 2:
        return (SPLITS[part][0], c1 - c0)
    return ((8 if stage == 0 else 2) * (r1 - r0) + 16, c1 - c0)


def half_type(stage):
    return jnp.float32 if stage == 2 else jnp.int16


LEVELS = 32767.0


def scatter_kernel(slot_ref, parts_ref, grad_ref, acc, outbox, inbox, *rest):
    landed = rest[:9]
    packed = rest[9:15]
    send, recv, pair_send, pair_recv = rest[15:]
    place = Place()
    edge = parts_ref.shape[1]

    def spans(part, stage, k, half):
        order = ORDERS[part]
        (r0, r1), (c0, c1) = CUTS[part]
        index = [slice(0, RING)] * 3
        for axis in order[:stage]:
            index[axis] = 0
        index[order[stage]] = k
        if half is not None:
            if stage < 2:
                index[order[stage + 1]] = slice(2 * half, 2 * half + 2)
            else:
                cut = r0 + SPLITS[part][0]
                r0, r1 = (r0, cut) if half == 0 else (cut, r1)
        return index, slice(r0, r1), slice(c0, c1)

    def region(ref, part, stage, k, half):
        index, rows, cols = spans(part, stage, k, half)
        return ref.at[index[0], index[1], index[2], rows, cols]

    def cells(part, stage, k, half):
        index, rows, cols = spans(part, stage, k, half)
        each = [range(i.start, i.stop) if isinstance(i, slice) else (i,) for i in index]
        return [acc.at[x, y, z, rows, cols] for x in each[0] for y in each[1] for z in each[2]]

    def half_of(way, k):
        return way if k != 1 else 1 - way

    def landing(part, stage, way, k):
        ref = landed[part * 3 + stage].at[way, k]
        if stage == 2:
            ref = ref.at[0 : SPLITS[part][half_of(way, k)]]
        return ref

    def source(part, stage, way, k):
        if stage < 2:
            return packed[part * 2 + stage].at[way, k]
        return region(acc, part, stage, 2 if k == 0 else (3 if way == 0 else 1), half_of(way, k))

    def transfer(part, stage, way, k):
        device = place.neighbour(ORDERS[part][stage], -1 if way == 0 else 1)
        at = (part, stage, way, k)
        return remote(
            source(part, stage, way, k), landing(part, stage, way, k), send.at[at], recv.at[at], device
        )

    def emit(part, stage, way, k):
        if stage < 2:
            refs = cells(part, stage, 2 if k == 0 else (3 if way == 0 else 1), half_of(way, k))
            rows = refs[0].shape[0]
            peak = jnp.abs(refs[0][...])
            for ref in refs[1:]:
                peak = jnp.maximum(peak, jnp.abs(ref[...]))
            peak = jnp.maximum(jnp.max(peak, axis=0, keepdims=True), 1e-30)
            power = jnp.ceil(jnp.log2(peak))
            factor = jnp.exp2(-power) * LEVELS
            out = source(part, stage, way, k)
            for i in range(0, len(refs), 2):
                both = jnp.concatenate([refs[i][...], refs[i + 1][...]], axis=0)
                out[i * rows : (i + 2) * rows, :] = (
                    jnp.round(both * factor).astype(jnp.int32).astype(jnp.int16)
                )
            out[len(refs) * rows :, :] = jnp.broadcast_to(
                power, (16, power.shape[1])
            ).astype(jnp.int32).astype(jnp.int16)
        transfer(part, stage, way, k).start()

    def take(part, stage, way, k):
        transfer(part, stage, way, k).wait_recv()
        refs = cells(part, stage, (3 if way == 0 else 1) if k == 0 else 0, half_of(way, k))
        came = landing(part, stage, way, k)
        if stage == 2:
            refs[0][...] = refs[0][...] + came[...]
            return
        rows = refs[0].shape[0]
        power = came[len(refs) * rows :, :].astype(jnp.int32).astype(jnp.float32)[:1]
        factor = jnp.exp2(power) * (1.0 / LEVELS)
        for i in range(0, len(refs), 2):
            both = came[i * rows : (i + 2) * rows, :].astype(jnp.int32).astype(jnp.float32) * factor
            refs[i][...] = refs[i][...] + both[:rows]
            refs[i + 1][...] = refs[i + 1][...] + both[rows:]

    def across(part, k):
        at = (part, k)
        return remote(
            region(outbox, part, 0, k, None),
            region(inbox, part, 0, k, None),
            pair_send.at[at],
            pair_recv.at[at],
            place.partner(),
        )

    def take_across(part, k):
        across(part, k).wait_recv()
        target = region(acc, part, 0, k, None)
        target[...] = target[...] + region(inbox, part, 0, k, None)[...]

    def spread(ref, core):
        @pl.loop(0, RING**3)
        def _(r):
            step = (lax.div(r, 16), lax.rem(lax.div(r, 4), 4), lax.rem(r, 4))
            blk, grp = place.device(
                [lax.rem(v + s, RING) for v, s in zip(place.coord, step)], core
            )
            first = (blk * 4 + grp) * 2
            for j in range(2):
                ref[step[0], step[1], step[2], j * edge : (j + 1) * edge, :] = parts_ref[
                    slot_ref[first + j]
                ]

    def sent(part, stage):
        for way in range(2):
            for k in range(3):
                transfer(part, stage, way, k).wait_send()

    place.announce()
    spread(outbox, 1 - place.core)
    place.await_peers()
    for k in (2, 3, 1, 0):
        for part in range(3):
            across(part, k).start()
    spread(acc, place.core)
    for part in range(3):
        take_across(part, 2)
        for way in range(2):
            emit(part, 0, way, 0)
    for part in range(3):
        for way, k in ((0, 3), (1, 1)):
            take_across(part, k)
            emit(part, 0, way, 1)
    for stage in range(3):
        for part in range(3):
            for way in range(2):
                take(part, stage, way, 0)
                emit(part, stage, way, 2)
        if stage == 0:
            for part in range(3):
                take_across(part, 0)
        if stage == 2:
            for part in range(3):
                for k in range(4):
                    across(part, k).wait_send()
                for before in range(2):
                    sent(part, before)
        for part in range(3):
            for k in (1, 2):
                for way in range(2):
                    take(part, stage, way, k)
            if stage < 2:
                for k in range(2):
                    for way in range(2):
                        emit(part, stage + 1, way, k)
    grad_ref[...] = acc[0, 0, 0]
    for part in range(3):
        sent(part, 2)


def scatter_gradients(parts, slot_of):
    edge, rank = parts.shape[1:]
    dense = (RING, RING, RING, 2 * edge, rank)
    buffers = [
        pltpu.VMEM((2, 3) + half_shape(part, stage), half_type(stage))
        for stages in (range(3), range(2))
        for part in range(3)
        for stage in stages
    ]
    return pl.pallas_call(
        scatter_kernel,
        out_shape=jax.ShapeDtypeStruct((2 * edge, rank), jnp.float32),
        in_specs=[
            pl.BlockSpec(memory_space=pltpu.SMEM),
            pl.BlockSpec(memory_space=pltpu.VMEM),
        ],
        out_specs=pl.BlockSpec(memory_space=pltpu.VMEM),
        scratch_shapes=[pltpu.VMEM(dense, jnp.float32)] * 3
        + buffers
        + [
            pltpu.SemaphoreType.DMA((3, 3, 2, 3)),
            pltpu.SemaphoreType.DMA((3, 3, 2, 3)),
            pltpu.SemaphoreType.DMA((3, 4)),
            pltpu.SemaphoreType.DMA((3, 4)),
        ],
        compiler_params=pltpu.CompilerParams(
            collective_id=1, has_side_effects=True, vmem_limit_bytes=62 << 20
        ),
    )(slot_of, parts)


def per_device(tensor_blocks, block_coords, block_count, row_owner, factors, moment1, moment2):
    edge = tensor_blocks.shape[1]
    modes, local_rows, rank = factors.shape
    local_blocks = local_rows // edge
    positions = lax.axis_size(AXES) * local_blocks
    table = gather_rows(factors).reshape(modes * positions, edge, rank)
    parts, slot_of = block_gradients(
        tensor_blocks, table, block_coords, row_owner, block_count, positions, local_blocks
    )
    grad = scatter_gradients(parts, slot_of)
    new_moment1 = 0.9 * moment1 + 0.1 * grad
    new_moment2 = 0.999 * moment2 + 0.001 * grad * grad
    new_factor = factors[0] - 0.02 * (new_moment1 / (1.0 - 0.9**8)) / (
        jnp.sqrt(new_moment2 / (1.0 - 0.999**8)) + 1e-08
    )
    return (new_factor, new_moment1, new_moment2)


def solution(mesh):
    return jax.shard_map(
        per_device,
        mesh=mesh,
        in_specs=(
            P(AXES, None, None),
            P(None, AXES),
            P(AXES),
            P(),
            P(None, AXES, None),
            P(AXES, None),
            P(AXES, None),
        ),
        out_specs=(P(AXES, None), P(AXES, None), P(AXES, None)),
        check_vma=False,
    )
```

```python
import functools

import jax
import jax.numpy as jnp
from jax import lax
from jax.experimental import pallas as pl
from jax.experimental.pallas import tpu as pltpu
from jax.sharding import PartitionSpec as P

AXES = ("blk", "grp")
MESH = pl.DeviceIdType.MESH
RING = 4
ORDERS = ((0, 1, 2), (1, 2, 0), (2, 0, 1))


class Place:
    def __init__(self):
        blk = lax.axis_index("blk")
        self.coord = [lax.div(blk, 8), lax.rem(lax.div(blk, 2), 4), lax.axis_index("grp")]
        self.core = lax.rem(blk, 2)

    @staticmethod
    def device(coord, core):
        return (coord[0] * 8 + coord[1] * 2 + core, coord[2])

    def partner(self):
        return self.device(self.coord, 1 - self.core)

    def along(self, axis, step):
        return lax.rem(self.coord[axis] + (RING + step), RING)

    def neighbour(self, axis, step):
        coord = list(self.coord)
        coord[axis] = self.along(axis, step)
        return self.device(coord, self.core)

    def offset(self, device):
        blk = device >> 2
        coord = (blk >> 3, (blk >> 1) & 3, device & 3)
        steps = [(v - me) & 3 for v, me in zip(coord, self.coord)]
        side = (blk ^ self.core) & 1
        return (steps[0] << 5) | (steps[1] << 3) | (steps[2] << 1) | side

    def announce(self):
        barrier = pltpu.get_barrier_semaphore()
        peers = [self.neighbour(axis, step) for axis in range(3) for step in (1, -1)]
        for peer in peers + [self.partner()]:
            pl.semaphore_signal(barrier, inc=1, device_id=peer, device_id_type=MESH)

    def await_peers(self):
        pl.semaphore_wait(pltpu.get_barrier_semaphore(), 7)


def remote(src, dst, send, recv, device):
    return pltpu.make_async_remote_copy(
        src_ref=src, dst_ref=dst, send_sem=send, recv_sem=recv, device_id=device, device_id_type=MESH
    )


ALL = slice(0, RING)
FAR = slice(1, RING)
GROUPS = (
    ((),),
    ((0,), (FAR,)),
    ((0, 0), (FAR, 0), (ALL, 1), (ALL, 3), (ALL, 2)),
)
LISTED = [(stage, g) for stage in range(3) for g in range(len(GROUPS[stage]))]
NUMBER = {at: i for i, at in enumerate(LISTED)}


def gather_kernel(own_ref, table_ref, cast_ref, local_sem, own_sem, send, recv, pair_send, pair_recv):
    place = Place()
    half_rows = cast_ref.shape[1] // 2

    def region(part, stage, g, value, half, side):
        index = [0, 0, 0]
        for axis, piece in zip(ORDERS[part], GROUPS[stage][g]):
            index[axis] = piece
        index[ORDERS[part][stage]] = value
        rows = slice(0, 2 * half_rows) if half is None else slice(half * half_rows, (half + 1) * half_rows)
        return table_ref.at[index[0], index[1], index[2], side, part, rows]

    def half_of(way, k):
        return way if k != 1 else 1 - way

    def copy(part, stage, g, way, k):
        half = half_of(way, k)
        came = 3 if way == 0 else 1
        if k == 2:
            src = region(part, stage, g, came, half, 0)
            dst = region(part, stage, g, 2, half, 0)
        else:
            src = region(part, stage, g, 0, half, 0)
            dst = region(part, stage, g, came, half, 0)
            if g == 0:
                src = cast_ref.at[part, half * half_rows : (half + 1) * half_rows]
        device = place.neighbour(ORDERS[part][stage], 1 if way == 0 else -1)
        at = (part, NUMBER[stage, g], way, k)
        return remote(src, dst, send.at[at], recv.at[at], device)

    def across(part, stage, g, way, j):
        value, half = ((3 if way == 0 else 1), None) if j == 0 else (2, way)
        at = (part, NUMBER[stage, g], way, j)
        return remote(
            region(part, stage, g, value, half, 0),
            region(part, stage, g, value, half, 1),
            pair_send.at[at],
            pair_recv.at[at],
            place.partner(),
        )

    steps = [(part, way) for part in range(3) for way in range(2)]

    def begin(stage, g):
        for k in range(2):
            for part, way in steps:
                copy(part, stage, g, way, k).start()

    def arrive(stage, g, k):
        for part, way in steps:
            copy(part, stage, g, way, k).wait_recv()
            if k == 0:
                copy(part, stage, g, way, 2).start()
            else:
                across(part, stage, g, way, k - 1).start()

    def drain(stage, g):
        for part, way in steps:
            for k in range(3):
                copy(part, stage, g, way, k).wait_send()
            for j in range(2):
                across(part, stage, g, way, j).wait_send()

    def collect(stage, g):
        for part, way in steps:
            for j in range(2):
                across(part, stage, g, way, j).wait_recv()

    place.announce()
    cast_ref[...] = own_ref[...].astype(cast_ref.dtype)
    place.await_peers()
    for stage in range(3):
        begin(stage, 0)
    mine = pltpu.make_async_copy(cast_ref, table_ref.at[0, 0, 0, 0], local_sem)
    mine.start()
    own = remote(cast_ref, table_ref.at[0, 0, 0, 1], own_sem.at[0], own_sem.at[1], place.partner())
    own.start()
    mine.wait()
    arrive(0, 0, 0)
    arrive(0, 0, 1)
    arrive(1, 0, 0)
    arrive(0, 0, 2)
    begin(1, 1)
    begin(2, 1)
    arrive(2, 0, 0)
    for k in range(1, 3):
        arrive(1, 0, k)
        arrive(2, 0, k)
    arrive(1, 1, 0)
    arrive(1, 1, 1)
    begin(2, 2)
    begin(2, 3)
    arrive(2, 1, 0)
    arrive(1, 1, 2)
    begin(2, 4)
    arrive(2, 1, 1)
    arrive(2, 1, 2)
    own.wait()
    for at in ((0, 0), (1, 0), (2, 0), (1, 1)):
        drain(*at)
        collect(*at)
    for g in (2, 3, 4):
        arrive(2, g, 0)
        arrive(2, g, 1)
    drain(2, 1)
    collect(2, 1)
    for g in (2, 3, 4):
        arrive(2, g, 2)
    for g in (2, 3, 4):
        drain(2, g)
        collect(2, g)


def gather_rows(factors):
    modes, rows, rank = factors.shape
    count = len(LISTED)
    return pl.pallas_call(
        gather_kernel,
        out_shape=jax.ShapeDtypeStruct((RING, RING, RING, 2, modes, rows, rank), jnp.bfloat16),
        in_specs=[pl.BlockSpec(memory_space=pltpu.VMEM)],
        out_specs=pl.BlockSpec(memory_space=pl.ANY),
        scratch_shapes=[
            pltpu.VMEM((modes, rows, rank), jnp.bfloat16),
            pltpu.SemaphoreType.DMA,
            pltpu.SemaphoreType.DMA((2,)),
            pltpu.SemaphoreType.DMA((3, count, 2, 3)),
            pltpu.SemaphoreType.DMA((3, count, 2, 3)),
            pltpu.SemaphoreType.DMA((3, count, 2, 2)),
            pltpu.SemaphoreType.DMA((3, count, 2, 2)),
        ],
        compiler_params=pltpu.CompilerParams(collective_id=0, has_side_effects=True),
    )(factors)


GROUP = 6
CHUNK = 16


def block_part(rows_ref, block_ref):
    _, edge, rank = rows_ref.shape
    half_a = rows_ref[0] * jnp.bfloat16(0.5)
    rows_c = rows_ref[2]
    width = CHUNK * edge
    twice = lambda rows: jnp.concatenate([rows, rows], axis=0).astype(jnp.float32).T
    cols_b = twice(rows_ref[1])
    cols_c = twice(rows_c).astype(jnp.bfloat16)
    lane = lax.broadcasted_iota(jnp.int32, (rank, 2 * edge), 1)
    total = jnp.zeros((edge, rank), jnp.float32)
    for step in range(edge // CHUNK):
        pair = jnp.concatenate(
            [rows_ref[1, pl.ds(step * CHUNK + j, 1), :] * rows_c for j in range(CHUNK)], axis=0
        )
        if step == 0:
            model = lax.dot_general(
                half_a, pair, (((1,), (1,)), ((), ())), preferred_element_type=jnp.float32
            )
        else:
            pieces = []
            for j in range(step * CHUNK, (step + 1) * CHUNK, 2):
                pick = jnp.where(lane < edge, j, j + 1)
                spread = jnp.take_along_axis(cols_b, pick, axis=1).astype(jnp.bfloat16)
                pieces.append(spread * cols_c)
            model = jnp.dot(
                half_a, jnp.concatenate(pieces, axis=1), preferred_element_type=jnp.float32
            )
        observed = block_ref[:, step * width : (step + 1) * width].astype(jnp.float32)
        resid = (0.5 * jnp.tanh(model) + (0.5 - observed)).astype(jnp.bfloat16)
        total = total + jnp.dot(resid, pair, preferred_element_type=jnp.float32)
    return total


def block_kernel(
    local_blocks, coords_ref, owner_ref, count_ref, blocks_ref, table_ref, parts_ref, slot_ref,
    block_buf, rows_buf, part_buf, block_sems, rows_sems, part_sems,
):
    slots = blocks_ref.shape[0]
    modes = rows_buf.shape[2]
    count = count_ref[0]
    place = Place()
    groups = lax.div(count + (GROUP - 1), GROUP)

    def block_copy(h, at):
        return pltpu.make_async_copy(
            blocks_ref.at[pl.ds(h * GROUP, GROUP)], block_buf.at[at], block_sems.at[at]
        )

    def start_rows(h, at, q):
        for m in range(modes):
            pos = owner_ref[m, coords_ref[m, h * GROUP + q]]
            row = (place.offset(pos >> 1) * modes + m) * local_blocks + (pos & 1)
            pltpu.make_async_copy(
                table_ref.at[row], rows_buf.at[at, q, m], rows_sems.at[at]
            ).start()

    def wait_rows(at):
        pltpu.make_async_copy(rows_buf.at[at], rows_buf.at[at], rows_sems.at[at]).wait()

    def store(h):
        span = pl.ds(h * GROUP, GROUP)
        return pltpu.make_async_copy(part_buf.at[span], parts_ref.at[span], part_sems.at[h])

    last = pltpu.make_async_copy(
        part_buf.at[slots], parts_ref.at[slots], part_sems.at[slots // GROUP]
    )

    block_copy(0, 0).start()

    for q in range(GROUP):
        start_rows(0, 0, q)

    @pl.loop(0, slot_ref.shape[0])
    def _(p):
        slot_ref[p] = slots

    @pl.loop(0, count)
    def _(s):
        slot_ref[owner_ref[0, coords_ref[0, s]]] = s

    part_buf[slots] = jnp.zeros(part_buf.shape[1:], jnp.float32)
    last.start()

    @pl.loop(0, groups)
    def _(h):
        at = lax.rem(h, 2)
        ahead = jnp.minimum(h + 1, groups - 1)
        block_copy(h, at).wait()
        wait_rows(at)
        block_copy(ahead, 1 - at).start()
        for q in range(GROUP):
            start_rows(ahead, 1 - at, q)
            part_buf[h * GROUP + q] = block_part(rows_buf.at[at, q], block_buf.at[at, q])
        store(h).start()

    @pl.loop(0, groups)
    def _(h):
        store(h).wait()

    last.wait()
    block_copy(0, lax.rem(groups, 2)).wait()
    wait_rows(lax.rem(groups, 2))


def block_gradients(tensor_blocks, table, coords, owner, count, positions, local_blocks):
    slots, edge, merged = tensor_blocks.shape
    modes, _ = coords.shape
    rank = table.shape[2]
    smem = pl.BlockSpec(memory_space=pltpu.SMEM)
    far = pl.BlockSpec(memory_space=pltpu.HBM)
    return pl.pallas_call(
        functools.partial(block_kernel, local_blocks),
        out_shape=(
            jax.ShapeDtypeStruct((slots + 1, edge, rank), jnp.float32),
            jax.ShapeDtypeStruct((positions,), jnp.int32),
        ),
        in_specs=[smem, smem, smem, far, far],
        out_specs=(far, smem),
        scratch_shapes=[
            pltpu.VMEM((2, GROUP, edge, merged), jnp.bfloat16),
            pltpu.VMEM((2, GROUP, modes, edge, rank), jnp.bfloat16),
            pltpu.VMEM((slots + 1, edge, rank), jnp.float32),
            pltpu.SemaphoreType.DMA((2,)),
            pltpu.SemaphoreType.DMA((2,)),
            pltpu.SemaphoreType.DMA((slots // GROUP + 1,)),
        ],
        compiler_params=pltpu.CompilerParams(vmem_limit_bytes=62 << 20),
        cost_estimate=pl.CostEstimate(
            flops=4 * slots * edge * merged * rank,
            bytes_accessed=2 * slots * edge * (merged + 5 * rank),
            transcendentals=slots * edge * merged,
        ),
    )(coords, owner, count, tensor_blocks, table)


CUTS = (((0, 88), (0, 128)), ((0, 88), (128, 256)), ((88, 128), (0, 256)))
SPLITS = ((48, 40), (48, 40), (24, 16))


def half_shape(part, stage):
    (r0, r1), (c0, c1) = CUTS[part]
    if stage == 2:
        return (SPLITS[part][0], c1 - c0)
    return ((8 if stage == 0 else 2) * (r1 - r0) + 16, c1 - c0)


def half_type(stage):
    return jnp.float32 if stage == 2 else jnp.int16


LEVELS = 32767.0


def scatter_kernel(slot_ref, parts_ref, grad_ref, acc, outbox, inbox, *rest):
    landed = rest[:9]
    packed = rest[9:15]
    send, recv, pair_send, pair_recv = rest[15:]
    place = Place()
    edge = parts_ref.shape[1]

    def spans(part, stage, k, half):
        order = ORDERS[part]
        (r0, r1), (c0, c1) = CUTS[part]
        index = [slice(0, RING)] * 3
        for axis in order[:stage]:
            index[axis] = 0
        index[order[stage]] = k
        if half is not None:
            if stage < 2:
                index[order[stage + 1]] = slice(2 * half, 2 * half + 2)
            else:
                cut = r0 + SPLITS[part][0]
                r0, r1 = (r0, cut) if half == 0 else (cut, r1)
        return index, slice(r0, r1), slice(c0, c1)

    def region(ref, part, stage, k, half):
        index, rows, cols = spans(part, stage, k, half)
        return ref.at[index[0], index[1], index[2], rows, cols]

    def cells(part, stage, k, half):
        index, rows, cols = spans(part, stage, k, half)
        each = [range(i.start, i.stop) if isinstance(i, slice) else (i,) for i in index]
        return [acc.at[x, y, z, rows, cols] for x in each[0] for y in each[1] for z in each[2]]

    def half_of(way, k):
        return way if k != 1 else 1 - way

    def landing(part, stage, way, k):
        ref = landed[part * 3 + stage].at[way, k]
        if stage == 2:
            ref = ref.at[0 : SPLITS[part][half_of(way, k)]]
        return ref

    def source(part, stage, way, k):
        if stage < 2:
            return packed[part * 2 + stage].at[way, k]
        return region(acc, part, stage, 2 if k == 0 else (3 if way == 0 else 1), half_of(way, k))

    def transfer(part, stage, way, k):
        device = place.neighbour(ORDERS[part][stage], -1 if way == 0 else 1)
        at = (part, stage, way, k)
        return remote(
            source(part, stage, way, k), landing(part, stage, way, k), send.at[at], recv.at[at], device
        )

    def emit(part, stage, way, k):
        if stage < 2:
            refs = cells(part, stage, 2 if k == 0 else (3 if way == 0 else 1), half_of(way, k))
            rows = refs[0].shape[0]
            peak = jnp.abs(refs[0][...])
            for ref in refs[1:]:
                peak = jnp.maximum(peak, jnp.abs(ref[...]))
            peak = jnp.maximum(jnp.max(peak, axis=0, keepdims=True), 1e-30)
            power = jnp.ceil(jnp.log2(peak))
            factor = jnp.exp2(-power) * LEVELS
            out = source(part, stage, way, k)
            for i in range(0, len(refs), 2):
                both = jnp.concatenate([refs[i][...], refs[i + 1][...]], axis=0)
                out[i * rows : (i + 2) * rows, :] = (
                    jnp.round(both * factor).astype(jnp.int32).astype(jnp.int16)
                )
            out[len(refs) * rows :, :] = jnp.broadcast_to(
                power, (16, power.shape[1])
            ).astype(jnp.int32).astype(jnp.int16)
        transfer(part, stage, way, k).start()

    def take(part, stage, way, k):
        transfer(part, stage, way, k).wait_recv()
        refs = cells(part, stage, (3 if way == 0 else 1) if k == 0 else 0, half_of(way, k))
        came = landing(part, stage, way, k)
        if stage == 2:
            refs[0][...] = refs[0][...] + came[...]
            return
        rows = refs[0].shape[0]
        power = came[len(refs) * rows :, :].astype(jnp.int32).astype(jnp.float32)[:1]
        factor = jnp.exp2(power) * (1.0 / LEVELS)
        for i in range(0, len(refs), 2):
            both = came[i * rows : (i + 2) * rows, :].astype(jnp.int32).astype(jnp.float32) * factor
            refs[i][...] = refs[i][...] + both[:rows]
            refs[i + 1][...] = refs[i + 1][...] + both[rows:]

    def across(part, k):
        at = (part, k)
        return remote(
            region(outbox, part, 0, k, None),
            region(inbox, part, 0, k, None),
            pair_send.at[at],
            pair_recv.at[at],
            place.partner(),
        )

    def take_across(part, k):
        across(part, k).wait_recv()
        target = region(acc, part, 0, k, None)
        target[...] = target[...] + region(inbox, part, 0, k, None)[...]

    def spread(ref, core):
        @pl.loop(0, RING**3)
        def _(r):
            step = (lax.div(r, 16), lax.rem(lax.div(r, 4), 4), lax.rem(r, 4))
            blk, grp = place.device(
                [lax.rem(v + s, RING) for v, s in zip(place.coord, step)], core
            )
            first = (blk * 4 + grp) * 2
            for j in range(2):
                ref[step[0], step[1], step[2], j * edge : (j + 1) * edge, :] = parts_ref[
                    slot_ref[first + j]
                ]

    def sent(part, stage):
        for way in range(2):
            for k in range(3):
                transfer(part, stage, way, k).wait_send()

    place.announce()
    spread(outbox, 1 - place.core)
    place.await_peers()
    for k in (2, 3, 1, 0):
        for part in range(3):
            across(part, k).start()
    spread(acc, place.core)
    for part in range(3):
        take_across(part, 2)
        for way in range(2):
            emit(part, 0, way, 0)
    for part in range(3):
        for way, k in ((0, 3), (1, 1)):
            take_across(part, k)
            emit(part, 0, way, 1)
    for stage in range(3):
        for part in range(3):
            for way in range(2):
                take(part, stage, way, 0)
                emit(part, stage, way, 2)
        if stage == 0:
            for part in range(3):
                take_across(part, 0)
        if stage == 2:
            for part in range(3):
                for k in range(4):
                    across(part, k).wait_send()
                for before in range(2):
                    sent(part, before)
        for part in range(3):
            for k in (1, 2):
                for way in range(2):
                    take(part, stage, way, k)
            if stage < 2:
                for k in range(2):
                    for way in range(2):
                        emit(part, stage + 1, way, k)
    grad_ref[...] = acc[0, 0, 0]
    for part in range(3):
        sent(part, 2)


def scatter_gradients(parts, slot_of):
    edge, rank = parts.shape[1:]
    dense = (RING, RING, RING, 2 * edge, rank)
    buffers = [
        pltpu.VMEM((2, 3) + half_shape(part, stage), half_type(stage))
        for stages in (range(3), range(2))
        for part in range(3)
        for stage in stages
    ]
    return pl.pallas_call(
        scatter_kernel,
        out_shape=jax.ShapeDtypeStruct((2 * edge, rank), jnp.float32),
        in_specs=[
            pl.BlockSpec(memory_space=pltpu.SMEM),
            pl.BlockSpec(memory_space=pltpu.VMEM),
        ],
        out_specs=pl.BlockSpec(memory_space=pltpu.VMEM),
        scratch_shapes=[pltpu.VMEM(dense, jnp.float32)] * 3
        + buffers
        + [
            pltpu.SemaphoreType.DMA((3, 3, 2, 3)),
            pltpu.SemaphoreType.DMA((3, 3, 2, 3)),
            pltpu.SemaphoreType.DMA((3, 4)),
            pltpu.SemaphoreType.DMA((3, 4)),
        ],
        compiler_params=pltpu.CompilerParams(
            collective_id=1, has_side_effects=True, vmem_limit_bytes=62 << 20
        ),
    )(slot_of, parts)


def per_device(tensor_blocks, block_coords, block_count, row_owner, factors, moment1, moment2):
    edge = tensor_blocks.shape[1]
    modes, local_rows, rank = factors.shape
    local_blocks = local_rows // edge
    positions = lax.axis_size(AXES) * local_blocks
    table = gather_rows(factors).reshape(modes * positions, edge, rank)
    parts, slot_of = block_gradients(
        tensor_blocks, table, block_coords, row_owner, block_count, positions, local_blocks
    )
    grad = scatter_gradients(parts, slot_of)
    new_moment1 = 0.9 * moment1 + 0.1 * grad
    new_moment2 = 0.999 * moment2 + 0.001 * grad * grad
    new_factor = factors[0] - 0.02 * (new_moment1 / (1.0 - 0.9**8)) / (
        jnp.sqrt(new_moment2 / (1.0 - 0.999**8)) + 1e-08
    )
    return (new_factor, new_moment1, new_moment2)


def solution(mesh):
    return jax.shard_map(
        per_device,
        mesh=mesh,
        in_specs=(
            P(AXES, None, None),
            P(None, AXES),
            P(AXES),
            P(),
            P(None, AXES, None),
            P(AXES, None),
            P(AXES, None),
        ),
        out_specs=(P(AXES, None), P(AXES, None), P(AXES, None)),
        check_vma=False,
    )
```

```python
import functools

import jax
import jax.numpy as jnp
from jax import lax
from jax.experimental import pallas as pl
from jax.experimental.pallas import tpu as pltpu
from jax.sharding import PartitionSpec as P

AXES = ("blk", "grp")
MESH = pl.DeviceIdType.MESH
RING = 4
ORDERS = ((0, 1, 2), (1, 2, 0), (2, 0, 1))


class Place:
    def __init__(self):
        blk = lax.axis_index("blk")
        self.coord = [lax.div(blk, 8), lax.rem(lax.div(blk, 2), 4), lax.axis_index("grp")]
        self.core = lax.rem(blk, 2)

    @staticmethod
    def device(coord, core):
        return (coord[0] * 8 + coord[1] * 2 + core, coord[2])

    def partner(self):
        return self.device(self.coord, 1 - self.core)

    def along(self, axis, step):
        return lax.rem(self.coord[axis] + (RING + step), RING)

    def neighbour(self, axis, step):
        coord = list(self.coord)
        coord[axis] = self.along(axis, step)
        return self.device(coord, self.core)

    def offset(self, device):
        blk = device >> 2
        coord = (blk >> 3, (blk >> 1) & 3, device & 3)
        steps = [(v - me) & 3 for v, me in zip(coord, self.coord)]
        side = (blk ^ self.core) & 1
        return (steps[0] << 5) | (steps[1] << 3) | (steps[2] << 1) | side

    def announce(self):
        barrier = pltpu.get_barrier_semaphore()
        peers = [self.neighbour(axis, step) for axis in range(3) for step in (1, -1)]
        for peer in peers + [self.partner()]:
            pl.semaphore_signal(barrier, inc=1, device_id=peer, device_id_type=MESH)

    def await_peers(self):
        pl.semaphore_wait(pltpu.get_barrier_semaphore(), 7)


def remote(src, dst, send, recv, device):
    return pltpu.make_async_remote_copy(
        src_ref=src, dst_ref=dst, send_sem=send, recv_sem=recv, device_id=device, device_id_type=MESH
    )


ALL = slice(0, RING)
FAR = slice(1, RING)
GROUPS = (
    ((),),
    ((0,), (FAR,)),
    ((0, 0), (FAR, 0), (ALL, 1), (ALL, 3), (ALL, 2)),
)
LISTED = [(stage, g) for stage in range(3) for g in range(len(GROUPS[stage]))]
NUMBER = {at: i for i, at in enumerate(LISTED)}


def gather_kernel(own_ref, table_ref, cast_ref, local_sem, own_sem, send, recv, pair_send, pair_recv):
    place = Place()
    half_rows = cast_ref.shape[1] // 2

    def region(part, stage, g, value, half, side):
        index = [0, 0, 0]
        for axis, piece in zip(ORDERS[part], GROUPS[stage][g]):
            index[axis] = piece
        index[ORDERS[part][stage]] = value
        rows = slice(0, 2 * half_rows) if half is None else slice(half * half_rows, (half + 1) * half_rows)
        return table_ref.at[index[0], index[1], index[2], side, part, rows]

    def half_of(way, k):
        return way if k != 1 else 1 - way

    def copy(part, stage, g, way, k):
        half = half_of(way, k)
        came = 3 if way == 0 else 1
        if k == 2:
            src = region(part, stage, g, came, half, 0)
            dst = region(part, stage, g, 2, half, 0)
        else:
            src = region(part, stage, g, 0, half, 0)
            dst = region(part, stage, g, came, half, 0)
            if g == 0:
                src = cast_ref.at[part, half * half_rows : (half + 1) * half_rows]
        device = place.neighbour(ORDERS[part][stage], 1 if way == 0 else -1)
        at = (part, NUMBER[stage, g], way, k)
        return remote(src, dst, send.at[at], recv.at[at], device)

    def across(part, stage, g, way, j):
        value, half = ((3 if way == 0 else 1), None) if j == 0 else (2, way)
        at = (part, NUMBER[stage, g], way, j)
        return remote(
            region(part, stage, g, value, half, 0),
            region(part, stage, g, value, half, 1),
            pair_send.at[at],
            pair_recv.at[at],
            place.partner(),
        )

    steps = [(part, way) for part in range(3) for way in range(2)]

    def begin(stage, g):
        for k in range(2):
            for part, way in steps:
                copy(part, stage, g, way, k).start()

    def arrive(stage, g, k):
        for part, way in steps:
            copy(part, stage, g, way, k).wait_recv()
            if k == 0:
                copy(part, stage, g, way, 2).start()
            else:
                across(part, stage, g, way, k - 1).start()

    def drain(stage, g):
        for part, way in steps:
            for k in range(3):
                copy(part, stage, g, way, k).wait_send()
            for j in range(2):
                across(part, stage, g, way, j).wait_send()

    def collect(stage, g):
        for part, way in steps:
            for j in range(2):
                across(part, stage, g, way, j).wait_recv()

    place.announce()
    cast_ref[...] = own_ref[...].astype(cast_ref.dtype)
    place.await_peers()
    for stage in range(3):
        begin(stage, 0)
    mine = pltpu.make_async_copy(cast_ref, table_ref.at[0, 0, 0, 0], local_sem)
    mine.start()
    own = remote(cast_ref, table_ref.at[0, 0, 0, 1], own_sem.at[0], own_sem.at[1], place.partner())
    own.start()
    arrive(0, 0, 0)
    arrive(0, 0, 1)
    arrive(1, 0, 0)
    arrive(0, 0, 2)
    begin(1, 1)
    begin(2, 1)
    arrive(2, 0, 0)
    for k in range(1, 3):
        arrive(1, 0, k)
        arrive(2, 0, k)
    arrive(1, 1, 0)
    arrive(1, 1, 1)
    begin(2, 2)
    begin(2, 3)
    arrive(2, 1, 0)
    arrive(1, 1, 2)
    begin(2, 4)
    arrive(2, 1, 1)
    arrive(2, 1, 2)
    mine.wait()
    own.wait()
    for at in ((0, 0), (1, 0), (2, 0), (1, 1)):
        drain(*at)
        collect(*at)
    for g in (2, 3, 4):
        arrive(2, g, 0)
        arrive(2, g, 1)
    drain(2, 1)
    collect(2, 1)
    for g in (2, 3, 4):
        arrive(2, g, 2)
    for g in (2, 3, 4):
        drain(2, g)
        collect(2, g)


def gather_rows(factors):
    modes, rows, rank = factors.shape
    count = len(LISTED)
    return pl.pallas_call(
        gather_kernel,
        out_shape=jax.ShapeDtypeStruct((RING, RING, RING, 2, modes, rows, rank), jnp.bfloat16),
        in_specs=[pl.BlockSpec(memory_space=pltpu.VMEM)],
        out_specs=pl.BlockSpec(memory_space=pl.ANY),
        scratch_shapes=[
            pltpu.VMEM((modes, rows, rank), jnp.bfloat16),
            pltpu.SemaphoreType.DMA,
            pltpu.SemaphoreType.DMA((2,)),
            pltpu.SemaphoreType.DMA((3, count, 2, 3)),
            pltpu.SemaphoreType.DMA((3, count, 2, 3)),
            pltpu.SemaphoreType.DMA((3, count, 2, 2)),
            pltpu.SemaphoreType.DMA((3, count, 2, 2)),
        ],
        compiler_params=pltpu.CompilerParams(collective_id=0, has_side_effects=True),
    )(factors)


GROUP = 6
CHUNK = 16


def block_part(rows_ref, block_ref):
    _, edge, rank = rows_ref.shape
    half_a = rows_ref[0] * jnp.bfloat16(0.5)
    rows_c = rows_ref[2]
    width = CHUNK * edge
    twice = lambda rows: jnp.concatenate([rows, rows], axis=0).astype(jnp.float32).T
    cols_b = twice(rows_ref[1])
    cols_c = twice(rows_c).astype(jnp.bfloat16)
    lane = lax.broadcasted_iota(jnp.int32, (rank, 2 * edge), 1)
    total = jnp.zeros((edge, rank), jnp.float32)
    for step in range(edge // CHUNK):
        pair = jnp.concatenate(
            [rows_ref[1, pl.ds(step * CHUNK + j, 1), :] * rows_c for j in range(CHUNK)], axis=0
        )
        if step == 0:
            model = lax.dot_general(
                half_a, pair, (((1,), (1,)), ((), ())), preferred_element_type=jnp.float32
            )
        else:
            pieces = []
            for j in range(step * CHUNK, (step + 1) * CHUNK, 2):
                pick = jnp.where(lane < edge, j, j + 1)
                spread = jnp.take_along_axis(cols_b, pick, axis=1).astype(jnp.bfloat16)
                pieces.append(spread * cols_c)
            model = jnp.dot(
                half_a, jnp.concatenate(pieces, axis=1), preferred_element_type=jnp.float32
            )
        observed = block_ref[:, step * width : (step + 1) * width].astype(jnp.float32)
        resid = (0.5 * jnp.tanh(model) + (0.5 - observed)).astype(jnp.bfloat16)
        total = total + jnp.dot(resid, pair, preferred_element_type=jnp.float32)
    return total


def block_kernel(
    local_blocks, coords_ref, owner_ref, count_ref, blocks_ref, table_ref, parts_ref, slot_ref,
    block_buf, rows_buf, part_buf, block_sems, rows_sems, part_sems,
):
    slots = blocks_ref.shape[0]
    modes = rows_buf.shape[2]
    count = count_ref[0]
    place = Place()
    groups = lax.div(count + (GROUP - 1), GROUP)

    def block_copy(h, at):
        return pltpu.make_async_copy(
            blocks_ref.at[pl.ds(h * GROUP, GROUP)], block_buf.at[at], block_sems.at[at]
        )

    def start_rows(h, at, q):
        for m in range(modes):
            pos = owner_ref[m, coords_ref[m, h * GROUP + q]]
            row = (place.offset(pos >> 1) * modes + m) * local_blocks + (pos & 1)
            pltpu.make_async_copy(
                table_ref.at[row], rows_buf.at[at, q, m], rows_sems.at[at]
            ).start()

    def wait_rows(at):
        pltpu.make_async_copy(rows_buf.at[at], rows_buf.at[at], rows_sems.at[at]).wait()

    def store(h):
        span = pl.ds(h * GROUP, GROUP)
        return pltpu.make_async_copy(part_buf.at[span], parts_ref.at[span], part_sems.at[h])

    last = pltpu.make_async_copy(
        part_buf.at[slots], parts_ref.at[slots], part_sems.at[slots // GROUP]
    )

    block_copy(0, 0).start()

    for q in range(GROUP):
        start_rows(0, 0, q)

    @pl.loop(0, slot_ref.shape[0], unroll=8)
    def _(p):
        slot_ref[p] = slots

    @pl.loop(0, count)
    def _(s):
        slot_ref[owner_ref[0, coords_ref[0, s]]] = s

    part_buf[slots] = jnp.zeros(part_buf.shape[1:], jnp.float32)
    last.start()

    @pl.loop(0, groups)
    def _(h):
        at = lax.rem(h, 2)
        ahead = jnp.minimum(h + 1, groups - 1)
        block_copy(h, at).wait()
        wait_rows(at)
        block_copy(ahead, 1 - at).start()
        for q in range(GROUP):
            start_rows(ahead, 1 - at, q)
            part_buf[h * GROUP + q] = block_part(rows_buf.at[at, q], block_buf.at[at, q])
        store(h).start()

    @pl.loop(0, groups)
    def _(h):
        store(h).wait()

    last.wait()
    block_copy(0, lax.rem(groups, 2)).wait()
    wait_rows(lax.rem(groups, 2))


def block_gradients(tensor_blocks, table, coords, owner, count, positions, local_blocks):
    slots, edge, merged = tensor_blocks.shape
    modes, _ = coords.shape
    rank = table.shape[2]
    smem = pl.BlockSpec(memory_space=pltpu.SMEM)
    far = pl.BlockSpec(memory_space=pltpu.HBM)
    return pl.pallas_call(
        functools.partial(block_kernel, local_blocks),
        out_shape=(
            jax.ShapeDtypeStruct((slots + 1, edge, rank), jnp.float32),
            jax.ShapeDtypeStruct((positions,), jnp.int32),
        ),
        in_specs=[smem, smem, smem, far, far],
        out_specs=(far, smem),
        scratch_shapes=[
            pltpu.VMEM((2, GROUP, edge, merged), jnp.bfloat16),
            pltpu.VMEM((2, GROUP, modes, edge, rank), jnp.bfloat16),
            pltpu.VMEM((slots + 1, edge, rank), jnp.float32),
            pltpu.SemaphoreType.DMA((2,)),
            pltpu.SemaphoreType.DMA((2,)),
            pltpu.SemaphoreType.DMA((slots // GROUP + 1,)),
        ],
        compiler_params=pltpu.CompilerParams(vmem_limit_bytes=62 << 20),
        cost_estimate=pl.CostEstimate(
            flops=4 * slots * edge * merged * rank,
            bytes_accessed=2 * slots * edge * (merged + 5 * rank),
            transcendentals=slots * edge * merged,
        ),
    )(coords, owner, count, tensor_blocks, table)


CUTS = (((0, 88), (0, 128)), ((0, 88), (128, 256)), ((88, 128), (0, 256)))
SPLITS = ((48, 40), (48, 40), (24, 16))


def half_shape(part, stage):
    (r0, r1), (c0, c1) = CUTS[part]
    if stage == 2:
        return (SPLITS[part][0], c1 - c0)
    return ((8 if stage == 0 else 2) * (r1 - r0) + 16, c1 - c0)


def half_type(stage):
    return jnp.float32 if stage == 2 else jnp.int16


LEVELS = 32767.0


def scatter_kernel(slot_ref, parts_ref, grad_ref, acc, outbox, inbox, *rest):
    landed = rest[:9]
    packed = rest[9:15]
    send, recv, pair_send, pair_recv = rest[15:]
    place = Place()
    edge = parts_ref.shape[1]

    def spans(part, stage, k, half):
        order = ORDERS[part]
        (r0, r1), (c0, c1) = CUTS[part]
        index = [slice(0, RING)] * 3
        for axis in order[:stage]:
            index[axis] = 0
        index[order[stage]] = k
        if half is not None:
            if stage < 2:
                index[order[stage + 1]] = slice(2 * half, 2 * half + 2)
            else:
                cut = r0 + SPLITS[part][0]
                r0, r1 = (r0, cut) if half == 0 else (cut, r1)
        return index, slice(r0, r1), slice(c0, c1)

    def region(ref, part, stage, k, half):
        index, rows, cols = spans(part, stage, k, half)
        return ref.at[index[0], index[1], index[2], rows, cols]

    def cells(part, stage, k, half):
        index, rows, cols = spans(part, stage, k, half)
        each = [range(i.start, i.stop) if isinstance(i, slice) else (i,) for i in index]
        return [acc.at[x, y, z, rows, cols] for x in each[0] for y in each[1] for z in each[2]]

    def half_of(way, k):
        return way if k != 1 else 1 - way

    def landing(part, stage, way, k):
        ref = landed[part * 3 + stage].at[way, k]
        if stage == 2:
            ref = ref.at[0 : SPLITS[part][half_of(way, k)]]
        return ref

    def source(part, stage, way, k):
        if stage < 2:
            return packed[part * 2 + stage].at[way, k]
        return region(acc, part, stage, 2 if k == 0 else (3 if way == 0 else 1), half_of(way, k))

    def transfer(part, stage, way, k):
        device = place.neighbour(ORDERS[part][stage], -1 if way == 0 else 1)
        at = (part, stage, way, k)
        return remote(
            source(part, stage, way, k), landing(part, stage, way, k), send.at[at], recv.at[at], device
        )

    def emit(part, stage, way, k):
        if stage < 2:
            refs = cells(part, stage, 2 if k == 0 else (3 if way == 0 else 1), half_of(way, k))
            rows = refs[0].shape[0]
            peak = jnp.abs(refs[0][...])
            for ref in refs[1:]:
                peak = jnp.maximum(peak, jnp.abs(ref[...]))
            peak = jnp.maximum(jnp.max(peak, axis=0, keepdims=True), 1e-30)
            power = jnp.ceil(jnp.log2(peak))
            factor = jnp.exp2(-power) * LEVELS
            out = source(part, stage, way, k)
            for i in range(0, len(refs), 2):
                both = jnp.concatenate([refs[i][...], refs[i + 1][...]], axis=0)
                out[i * rows : (i + 2) * rows, :] = (
                    jnp.round(both * factor).astype(jnp.int32).astype(jnp.int16)
                )
            out[len(refs) * rows :, :] = jnp.broadcast_to(
                power, (16, power.shape[1])
            ).astype(jnp.int32).astype(jnp.int16)
        transfer(part, stage, way, k).start()

    def take(part, stage, way, k):
        transfer(part, stage, way, k).wait_recv()
        refs = cells(part, stage, (3 if way == 0 else 1) if k == 0 else 0, half_of(way, k))
        came = landing(part, stage, way, k)
        if stage == 2:
            refs[0][...] = refs[0][...] + came[...]
            return
        rows = refs[0].shape[0]
        power = came[len(refs) * rows :, :].astype(jnp.int32).astype(jnp.float32)[:1]
        factor = jnp.exp2(power) * (1.0 / LEVELS)
        for i in range(0, len(refs), 2):
            both = came[i * rows : (i + 2) * rows, :].astype(jnp.int32).astype(jnp.float32) * factor
            refs[i][...] = refs[i][...] + both[:rows]
            refs[i + 1][...] = refs[i + 1][...] + both[rows:]

    def across(part, k):
        at = (part, k)
        return remote(
            region(outbox, part, 0, k, None),
            region(inbox, part, 0, k, None),
            pair_send.at[at],
            pair_recv.at[at],
            place.partner(),
        )

    def take_across(part, k):
        across(part, k).wait_recv()
        target = region(acc, part, 0, k, None)
        target[...] = target[...] + region(inbox, part, 0, k, None)[...]

    def spread(ref, core):
        @pl.loop(0, RING**3)
        def _(r):
            step = (lax.div(r, 16), lax.rem(lax.div(r, 4), 4), lax.rem(r, 4))
            blk, grp = place.device(
                [lax.rem(v + s, RING) for v, s in zip(place.coord, step)], core
            )
            first = (blk * 4 + grp) * 2
            for j in range(2):
                ref[step[0], step[1], step[2], j * edge : (j + 1) * edge, :] = parts_ref[
                    slot_ref[first + j]
                ]

    def sent(part, stage):
        for way in range(2):
            for k in range(3):
                transfer(part, stage, way, k).wait_send()

    place.announce()
    spread(outbox, 1 - place.core)
    place.await_peers()
    for k in (2, 3, 1, 0):
        for part in range(3):
            across(part, k).start()
    spread(acc, place.core)
    for part in range(3):
        take_across(part, 2)
        for way in range(2):
            emit(part, 0, way, 0)
    for part in range(3):
        for way, k in ((0, 3), (1, 1)):
            take_across(part, k)
            emit(part, 0, way, 1)
    for stage in range(3):
        for part in range(3):
            for way in range(2):
                take(part, stage, way, 0)
                emit(part, stage, way, 2)
        if stage == 0:
            for part in range(3):
                take_across(part, 0)
        if stage == 2:
            for part in range(3):
                for k in range(4):
                    across(part, k).wait_send()
                for before in range(2):
                    sent(part, before)
        for part in range(3):
            for k in (1, 2):
                for way in range(2):
                    take(part, stage, way, k)
            if stage < 2:
                for k in range(2):
                    for way in range(2):
                        emit(part, stage + 1, way, k)
    grad_ref[...] = acc[0, 0, 0]
    for part in range(3):
        sent(part, 2)


def scatter_gradients(parts, slot_of):
    edge, rank = parts.shape[1:]
    dense = (RING, RING, RING, 2 * edge, rank)
    buffers = [
        pltpu.VMEM((2, 3) + half_shape(part, stage), half_type(stage))
        for stages in (range(3), range(2))
        for part in range(3)
        for stage in stages
    ]
    return pl.pallas_call(
        scatter_kernel,
        out_shape=jax.ShapeDtypeStruct((2 * edge, rank), jnp.float32),
        in_specs=[
            pl.BlockSpec(memory_space=pltpu.SMEM),
            pl.BlockSpec(memory_space=pltpu.VMEM),
        ],
        out_specs=pl.BlockSpec(memory_space=pltpu.VMEM),
        scratch_shapes=[pltpu.VMEM(dense, jnp.float32)] * 3
        + buffers
        + [
            pltpu.SemaphoreType.DMA((3, 3, 2, 3)),
            pltpu.SemaphoreType.DMA((3, 3, 2, 3)),
            pltpu.SemaphoreType.DMA((3, 4)),
            pltpu.SemaphoreType.DMA((3, 4)),
        ],
        compiler_params=pltpu.CompilerParams(
            collective_id=1, has_side_effects=True, vmem_limit_bytes=62 << 20
        ),
    )(slot_of, parts)


def per_device(tensor_blocks, block_coords, block_count, row_owner, factors, moment1, moment2):
    edge = tensor_blocks.shape[1]
    modes, local_rows, rank = factors.shape
    local_blocks = local_rows // edge
    positions = lax.axis_size(AXES) * local_blocks
    table = gather_rows(factors).reshape(modes * positions, edge, rank)
    parts, slot_of = block_gradients(
        tensor_blocks, table, block_coords, row_owner, block_count, positions, local_blocks
    )
    grad = scatter_gradients(parts, slot_of)
    new_moment1 = 0.9 * moment1 + 0.1 * grad
    new_moment2 = 0.999 * moment2 + 0.001 * grad * grad
    new_factor = factors[0] - 0.02 * (new_moment1 / (1.0 - 0.9**8)) / (
        jnp.sqrt(new_moment2 / (1.0 - 0.999**8)) + 1e-08
    )
    return (new_factor, new_moment1, new_moment2)


def solution(mesh):
    return jax.shard_map(
        per_device,
        mesh=mesh,
        in_specs=(
            P(AXES, None, None),
            P(None, AXES),
            P(AXES),
            P(),
            P(None, AXES, None),
            P(AXES, None),
            P(AXES, None),
        ),
        out_specs=(P(AXES, None), P(AXES, None), P(AXES, None)),
        check_vma=False,
    )
```
